32 devices in a mesh: dp: 8 (over y, x, core), mp: 4 (over z).
Axes of the slice: x: 2, y: 2, z: 4, core: 2. Of those that a mesh axis runs over, the one named last changes fastest.
Arguments:
- hidden: bfloat16 [4096, 768], P('dp'), may hold values from -6 to 6
- cotangent: bfloat16 [4096, 768], P('dp'), may hold values from -6 to 6
- seq_lens: int32 [8], P('dp'), may hold values from 1 to 512, 2560 in all
- w_qkv: bfloat16 [3, 768, 768], P(None, None, 'mp'), may hold values from -0.21875 to 0.21875
- b_qkv: float32 [3, 768], P(None, 'mp'), may hold values from -3 to 3
- w_out: bfloat16 [768, 768], P('mp'), may hold values from -3.5 to 3.5
- out_biases: float32 [2, 768], replicated, may hold values from -3 to 3
- w_up: bfloat16 [768, 3072], P(None, 'mp'), may hold values from -0.21875 to 0.21875
- b_up: float32 [3072], P('mp'), may hold values from -3 to 3
- w_down: bfloat16 [3072, 768], P('mp'), may hold values from -0.109375 to 0.109375
- rel_table: bfloat16 [512, 768], replicated, may hold values from -6 to 6
- norm_gains: float32 [2, 768], replicated, may hold values from 0.5 to 1.5
- norm_biases: float32 [2, 768], replicated, may hold values from -3 to 3
- rel_gain: float32 [768], replicated, may hold values from 0.5 to 1.5
- rel_bias: float32 [768], replicated, may hold values from -3 to 3
Outputs:
- output: bfloat16 [4096, 768], P(('dp', 'mp'))
- d_hidden: bfloat16 [4096, 768], P(('dp', 'mp'))
- d_w_qkv: float32 [3, 768, 768], P(None, None, 'mp')
- d_b_qkv: float32 [3, 768], P(None, 'mp')
- d_w_out: float32 [768, 768], P('mp')
- d_out_biases: float32 [2, 768], replicated
- d_w_up: float32 [768, 3072], P(None, 'mp')
- d_b_up: float32 [3072], P('mp')
- d_w_down: float32 [3072, 768], P('mp')
- d_rel_table: float32 [512, 768], P('mp')
- d_norm_gains: float32 [2, 768], replicated
- d_norm_biases: float32 [2, 768], replicated
- d_rel_gain: float32 [768], P('mp')
- d_rel_bias: float32 [768], P('mp')
The draws below stay inside these ranges and needn't reach their ends.
Inputs may be any that keep to these rules, and one draw needn't show every extreme that they name: Slot s holds one sequence of seq_lens[s] tokens at its start and padding after it; some slot holds exactly 512 tokens.
All inputs are finite; a program needn't handle non-finite values. No bound on the sum of `seq_lens` on one device may be relied on, other than what follows from the above.
Results may differ from the reference program's by a relative error of at most 0.02.
Values may be sent and summed in bfloat16 or wider, within the bound.
No kernel may reach another device: no remote copies, remote signals or barrier semaphores. Data moves between devices by JAX's collectives and lax.ppermute only.
A program may use at most 128 MiB of HBM per device.

```python
import math
import jax
import jax.numpy as jnp
import numpy as np
from jax import lax

D = 768
HEADS = 12
HEAD_DIM = 64
FF = 3072
BUCKETS = 256
SLOT = 512
SEQS = 8
TOKENS = 4096
TABLE = 512


def block_levels(rng, shape, pieces, smallest, high):
    loudness, own = 1.0, jax.random.fold_in(rng, 6)
    for position, parts in pieces:
        steps = jnp.exp(jax.random.uniform(jax.random.fold_in(own, position), (parts,), jnp.float32, smallest / len(pieces), high / len(pieces)))
        loudness = loudness * jnp.repeat(steps, shape[position] // parts).reshape([-1 if axis == position else 1 for axis in range(len(shape))])
    return loudness


def split_up(number_of, total, bound, slope):
    weights = [(1 << 20) // math.isqrt(grade ** slope) + 1 for grade in range(2, number_of + 1)]
    surplus, given = total - bound - (number_of - 1), [1] * (number_of - 1)
    while surplus > 0:
        candidates = [i for i in range(number_of - 1) if given[i] < bound]
        pool, remaining = sum([weights[i] for i in candidates]), surplus
        for i in candidates:
            addition = min(bound - given[i], max(1, remaining * weights[i] // pool), surplus)
            given[i] = given[i] + addition
            surplus = surplus - addition
    return np.array([bound] + given)


def ragged_sizes(key, count, total, bound, skew):
    if count == 2:
        one = jax.random.randint(key, (), max(1, total - bound), min(bound, total - 1) + 1)
        return jnp.stack([one, total - one])
    sizes = jnp.asarray(split_up(count, total, bound, skew), jnp.int32)
    couples = (count - 1) // 2
    source_of, taker = sizes[1:1 + 2 * couples:2], sizes[2:2 + 2 * couples:2]
    slack = jnp.minimum(source_of - 1, bound - taker)
    shifted = jax.random.randint(jax.random.fold_in(key, 1), (couples,), 0, 1 << 20) % (slack + 1)
    sizes = sizes.at[1:1 + 2 * couples:2].set(source_of - shifted).at[2:2 + 2 * couples:2].set(taker + shifted)
    return sizes[jax.random.permutation(jax.random.fold_in(key, 2), count)]


def centred(own_key, extent, spread, reach, shards=(), kind=jnp.bfloat16):
    array = spread * jax.random.normal(own_key, extent, jnp.float32)
    if shards:
        array = array * block_levels(own_key, extent, shards, -0.22, 0.18)
    return jnp.clip(array, -reach, reach).astype(kind)


def setup_inputs(seed: int = 0) -> dict:
    seeds = jax.random.split(jax.random.key(seed), 16)
    return {
        "hidden": centred(seeds[0], (TOKENS, D), 1.0, 6.0, ((0, 8),)),
        "cotangent": centred(seeds[1], (TOKENS, D), 1.0, 6.0, ((0, 8),)),
        "seq_lens": ragged_sizes(seeds[2], SEQS, SEQS * (5 * SLOT // 8), SLOT, 2).astype(jnp.int32),
        "w_qkv": centred(seeds[3], (3, D, D), D ** -0.5, 0.21875, ((2, 4),)),
        "b_qkv": centred(seeds[4], (3, D), 0.5, 3.0, ((1, 4),), jnp.float32),
        "w_out": centred(seeds[5], (D, D), (max(D // 256, 1)) ** -0.5, 3.5, ((0, 4),)),
        "out_biases": centred(seeds[6], (2, D), 0.5, 3.0, (), jnp.float32),
        "w_up": centred(seeds[7], (D, FF), D ** -0.5, 0.21875, ((1, 4),)),
        "b_up": centred(seeds[8], (FF,), 0.5, 3.0, ((0, 4),), jnp.float32),
        "w_down": centred(seeds[9], (FF, D), FF ** -0.5, 0.109375, ((0, 4),)),
        "rel_table": centred(seeds[10], (TABLE, D), 1.0, 6.0),
        "norm_gains": jnp.clip(1.0 + 0.1 * jax.random.normal(seeds[11], (2, D), jnp.float32), 0.5, 1.5),
        "norm_biases": centred(seeds[12], (2, D), 0.5, 3.0, (), jnp.float32),
        "rel_gain": jnp.clip(1.0 + 0.1 * jax.random.normal(seeds[13], (D,), jnp.float32), 0.5, 1.5),
        "rel_bias": centred(seeds[14], (D,), 0.5, 3.0, (), jnp.float32),
    }


EPSILON = 1e-07

@jax.custom_vjp
def low(v):
    return lax.optimization_barrier(v.astype(jnp.bfloat16)).astype(jnp.float32)

@jax.custom_vjp
def low_back(v):
    return v

def low_keep(v):
    return (low(v), None)

def low_pass(kept, grad):
    return (grad,)

def back_keep(v):
    return (v, None)

def back_low(kept, grad):
    return (low(grad),)
low.defvjp(low_keep, low_pass)
low_back.defvjp(back_keep, back_low)

def bucket_positions(span_len, buckets):
    middle = buckets // 2
    offsets = np.arange(-(span_len - 1), span_len)

    def bucket_of(relative):
        signs = np.sign(relative)
        magnitude = np.where((relative < middle) & (relative > -middle), middle - 1, np.abs(relative))
        logged = np.ceil(np.log(magnitude / middle) / np.log((span_len - 1) / middle) * (middle - 1)) + middle
        logged = np.minimum(logged, buckets - 1)
        return np.where(magnitude <= middle, relative, logged * signs).astype(np.int64)
    return (bucket_of(offsets) + buckets, bucket_of(-offsets) + buckets)

def to_relative(full_scores):
    n = full_scores.shape[-2]
    leading = full_scores.shape[:-2]
    flipped = jnp.flip(full_scores, -1)
    padded = jnp.pad(flipped, [(0, 0)] * len(leading) + [(0, 0), (0, 1)])
    flattened = padded.reshape(leading + (2 * n * n,))
    window_part = lax.slice_in_dim(flattened, n - 1, n - 1 + n * (2 * n - 1), axis=len(leading))
    return window_part.reshape(leading + (n, 2 * n - 1))[..., :n]

def layer_norm(values, gain_row, shift_row):
    centered = values - lax.optimization_barrier(jnp.mean(values, axis=-1, keepdims=True))
    inv_std = lax.rsqrt(lax.optimization_barrier(jnp.mean(centered * centered, axis=-1, keepdims=True)) + EPSILON)
    return centered * inv_std * gain_row + shift_row

def exact_dot(left, right):
    return jnp.dot(left, right, precision=lax.Precision.HIGHEST)

def reference(hidden, cotangent, seq_lens, w_qkv, b_qkv, w_out, out_biases, w_up, b_up, w_down, rel_table, norm_gains, norm_biases, rel_gain, rel_bias):
    forward_index, reverse_index = bucket_positions(SLOT, BUCKETS)
    forward_index = jnp.asarray(forward_index.astype(np.int32))
    reverse_index = jnp.asarray(reverse_index.astype(np.int32))
    score_scale = 1.0 / math.sqrt(3 * HEAD_DIM)
    highest = lax.Precision.HIGHEST

    def whole_layer(tokens, qkv_weight, qkv_bias, out_weight, out_bias, up_weight, up_bias, down_weight, table, gain_pair, bias_pair, table_gain, table_bias):
        table_low = low(layer_norm(table, table_gain, table_bias))
        query_pos = low(low_back(exact_dot(table_low, qkv_weight[0]) + qkv_bias[0]))
        key_pos = low(low_back(exact_dot(table_low, qkv_weight[1]) + qkv_bias[1]))
        key_table = jnp.take(key_pos, forward_index, axis=0).reshape(2 * SLOT - 1, HEADS, HEAD_DIM)
        query_table = jnp.take(query_pos, reverse_index, axis=0).reshape(2 * SLOT - 1, HEADS, HEAD_DIM)

        def one_slot(inputs):
            slot_rows, length = inputs
            valid_keys = jnp.arange(SLOT, dtype=jnp.int32) < length
            query_rows = low(low_back(exact_dot(slot_rows, qkv_weight[0]) + qkv_bias[0])).reshape(SLOT, HEADS, HEAD_DIM)
            key_rows = low(low_back(exact_dot(slot_rows, qkv_weight[1]) + qkv_bias[1])).reshape(SLOT, HEADS, HEAD_DIM)
            value_rows = low(low_back(exact_dot(slot_rows, qkv_weight[2]) + qkv_bias[2])).reshape(SLOT, HEADS, HEAD_DIM)
            content = jnp.einsum('ihd,jhd->hij', query_rows, key_rows, precision=highest)
            to_pos = jnp.einsum('ihd,ehd->hie', query_rows, key_table, precision=highest)
            from_pos = jnp.einsum('jhd,ehd->hje', key_rows, query_table, precision=highest)
            scores = low_back((content + to_relative(to_pos) + jnp.swapaxes(to_relative(from_pos), 1, 2)) * score_scale)
            scores = jnp.where(valid_keys[None, None, :], scores, -1e+30)
            row_peak = lax.optimization_barrier(jnp.max(scores, axis=2, keepdims=True))
            exponents = jnp.exp(scores - row_peak)
            probabilities = low(exponents / lax.optimization_barrier(jnp.sum(exponents, axis=2, keepdims=True)))
            context = jnp.einsum('hij,jhd->ihd', probabilities, value_rows, precision=highest).reshape(SLOT, D)
            context = low(low_back(context))
            attention = low_back(exact_dot(context, out_weight))
            first = layer_norm(slot_rows + attention + out_bias[0], gain_pair[0], bias_pair[0])
            pre_act = low_back(exact_dot(low(first), up_weight) + up_bias)
            feed_out = low_back(exact_dot(low(jax.nn.gelu(pre_act, approximate=False)), down_weight))
            second = layer_norm(first + feed_out + out_bias[1], gain_pair[1], bias_pair[1])
            return jnp.where(valid_keys[:, None], second, 0.0)
        outputs = lax.map(jax.checkpoint(one_slot), (tokens.reshape(SEQS, SLOT, D), seq_lens))
        return outputs.reshape(TOKENS, D)
    primals = (hidden.astype(jnp.float32), w_qkv.astype(jnp.float32), b_qkv, w_out.astype(jnp.float32), out_biases, w_up.astype(jnp.float32), b_up, w_down.astype(jnp.float32), rel_table.astype(jnp.float32), norm_gains, norm_biases, rel_gain, rel_bias)
    result, pullback = jax.vjp(whole_layer, *primals)
    grads = pullback(cotangent.astype(jnp.float32))
    return (result.astype(jnp.bfloat16), grads[0].astype(jnp.bfloat16), grads[1], grads[2], grads[3], grads[4], grads[5], grads[6], grads[7], grads[8], grads[9], grads[10], grads[11], grads[12])
```

```python
import functools
import math

import jax
import jax.numpy as jnp
import numpy as np
from jax import lax
from jax.experimental import pallas as pl
from jax.experimental.pallas import tpu as pltpu
from jax.sharding import PartitionSpec as P

HEAD_DIM = 64
SLOT = 512
BLK = 128
NB = SLOT // BLK
WIN = SLOT + BLK
EPS = 1e-07
INV_ROOT_TWO = 0.7071067811865476
INV_ROOT_TWO_PI = 0.3989422804014327
SCALE = 1.0 / math.sqrt(3 * HEAD_DIM)
TAIL = 16
BF = jnp.bfloat16
F32 = jnp.float32
VM = pl.BlockSpec(memory_space=pltpu.VMEM)
SM = pl.BlockSpec(memory_space=pltpu.SMEM)


def sds(shape, dtype):
    return jax.ShapeDtypeStruct(shape, dtype)


def bucket_index(span_len, buckets):
    middle = buckets // 2
    offsets = np.arange(-(span_len - 1), span_len)
    signs = np.sign(offsets)
    magnitude = np.where(
        (offsets < middle) & (offsets > -middle), middle - 1, np.abs(offsets)
    )
    logged = (
        np.ceil(np.log(magnitude / middle) / np.log((span_len - 1) / middle) * (middle - 1))
        + middle
    )
    logged = np.minimum(logged, buckets - 1)
    return np.where(magnitude <= middle, offsets, logged * signs).astype(np.int64) + buckets


def index_rows(buckets):
    by_offset = bucket_index(SLOT, buckets)
    entry = np.arange(2 * SLOT)

    def pick(r):
        return by_offset[np.clip(r, -(SLOT - 1), SLOT - 1) + SLOT - 1]

    return np.stack([pick(SLOT - 1 - entry), pick(entry - (SLOT - 1))]).astype(np.int32)


def mm(a, b, ca=1, cb=0):
    return lax.dot_general(a, b, (((ca,), (cb,)), ((), ())), preferred_element_type=F32)


def skew(x):
    return pltpu.roll(x, WIN - (BLK - 1), 1, stride=1, stride_axis=0)[:, :SLOT]


def unskew(x):
    padded = jnp.concatenate([x, jnp.zeros((BLK, BLK), x.dtype)], 1)
    return pltpu.roll(padded, 0, 1, stride=1, stride_axis=0)


def anti():
    a = lax.broadcasted_iota(jnp.int32, (BLK, BLK), 0)
    b = lax.broadcasted_iota(jnp.int32, (BLK, BLK), 1)
    return (a + b == BLK - 1).astype(F32).astype(BF)


def block(b):
    return slice(b * BLK, (b + 1) * BLK)


def moments(values):
    centered = values - jnp.mean(values, axis=-1, keepdims=True)
    inv_std = lax.rsqrt(jnp.mean(centered * centered, axis=-1, keepdims=True) + EPS)
    return centered * inv_std, inv_std


def norm_back(grad_in, normed, inv_std, gain_row):
    scaled = grad_in * gain_row
    return inv_std * (
        scaled
        - jnp.mean(scaled, axis=-1, keepdims=True)
        - normed * jnp.mean(scaled * normed, axis=-1, keepdims=True)
    )


def colsum(x):
    return jnp.sum(x, axis=0, keepdims=True)


def attn_fwd_kernel(
    len_ref, z_ref, hid_ref, w_ref, b_ref, tab_ref, tg_ref, tb_ref, idx_ref, wo_ref,
    ctx_ref, qkv_ref, tt_ref, pt_ref, own_ref, *rest, heads,
):
    send_refs = rest[: NB - 1]
    at_s, st_s, p_s = rest[NB - 1 :]
    normed, _ = moments(tab_ref[...].astype(F32))
    table_low = (normed * tg_ref[...] + tb_ref[...]).astype(BF)
    rows = table_low.shape[0]
    hid = hid_ref[...]
    flip = anti()
    for c in range(3):
        r = (mm(hid, w_ref[c]) + b_ref[c : c + 1, :]).astype(BF)
        for h in range(heads):
            qkv_ref[c, h] = r[:, h * HEAD_DIM : (h + 1) * HEAD_DIM]
        if c:
            for b in range(NB):
                back = mm(flip, r[block(NB - 1 - b)]).astype(BF)
                for h in range(heads):
                    qkv_ref[2 + c, h, block(b), :] = back[:, h * HEAD_DIM : (h + 1) * HEAD_DIM]
    pos = lax.broadcasted_iota(jnp.int32, (rows, 2 * SLOT), 0)
    key_query = [
        (mm(table_low, w_ref[1 - c]) + b_ref[1 - c : 2 - c, :]).astype(BF) for c in range(2)
    ]
    hot = [(pos == idx_ref[c : c + 1, :]).astype(F32).astype(BF) for c in range(2)]
    for c, (source, order) in enumerate(((0, 0), (1, 1), (0, 1))):
        spread = mm(key_query[source], hot[order], 0, 0).astype(BF)
        for h in range(heads):
            tt_ref[c, h] = spread[h * HEAD_DIM : (h + 1) * HEAD_DIM, :]
    length = len_ref[0]

    def head(h, carry):
        for b in range(NB):
            w = slice((NB - 1 - b) * BLK, (NB - 1 - b) * BLK + WIN)
            a = skew(mm(qkv_ref[0, h, block(b), :], tt_ref[0, h, :, w]))
            at_s[:, block(b)] = a.T
        q = qkv_ref[0, h]
        peak = None
        for b in range(NB):
            w = slice((NB - 1 - b) * BLK, (NB - 1 - b) * BLK + WIN)
            kb = qkv_ref[1, h, block(b), :]
            s = (mm(kb, q, 1, 1) + skew(mm(kb, tt_ref[1, h, :, w])) + at_s[block(b), :]) * SCALE
            j = lax.broadcasted_iota(jnp.int32, s.shape, 0) + b * BLK
            s = jnp.where(j < length, s, -1e30)
            st_s[block(b), :] = s
            m = jnp.max(s, axis=0, keepdims=True)
            peak = m if peak is None else jnp.maximum(peak, m)
        total = None
        for b in range(NB):
            e = jnp.exp(st_s[block(b), :] - peak)
            st_s[block(b), :] = e
            d = colsum(e)
            total = d if total is None else total + d
        share = 1.0 / total
        for b in range(NB):
            p = (st_s[block(b), :] * share).astype(BF)
            p_s[block(b), :] = p
            pt_ref[h, block(NB - 1 - b), :] = mm(flip, p).astype(BF)
        c = mm(qkv_ref[2, h], p_s[...], 0, 0)
        at_s[:, 0:HEAD_DIM] = c.T
        ctx_ref[h] = at_s[:, 0:HEAD_DIM].astype(BF)
        return carry

    lax.fori_loop(0, heads, head, 0)
    z = z_ref[0]
    for s in range(NB):
        rows = pl.ds(pl.multiple_of(((z + s) % NB) * BLK, BLK), BLK)
        part = mm(jnp.concatenate([ctx_ref[h, rows, :] for h in range(heads)], 1), wo_ref[...])
        if s == 0:
            own_ref[...] = part
        else:
            send_refs[s - 1][...] = part.astype(BF)


def attn_fwd(seq_len, z, hidden, w_qkv, b_qkv, rel_table, rel_gain, rel_bias, idx, w_out):
    heads = w_qkv.shape[2] // HEAD_DIM
    d = hidden.shape[1]
    return pl.pallas_call(
        functools.partial(attn_fwd_kernel, heads=heads),
        out_shape=(
            sds((heads, SLOT, HEAD_DIM), BF),
            sds((5, heads, SLOT, HEAD_DIM), BF),
            sds((3, heads, HEAD_DIM, 2 * SLOT), BF),
            sds((heads, SLOT, SLOT), BF),
            sds((BLK, d), F32),
        )
        + (sds((BLK, d), BF),) * (NB - 1),
        in_specs=[SM, SM] + [VM] * 8,
        out_specs=(VM,) * (4 + NB),
        scratch_shapes=[
            pltpu.VMEM((SLOT, SLOT), F32),
            pltpu.VMEM((SLOT, SLOT), F32),
            pltpu.VMEM((SLOT, SLOT), BF),
        ],
        name="attn_fwd",
    )(seq_len, z, hidden, w_qkv, b_qkv, rel_table, rel_gain, rel_bias, idx, w_out)


def first_norm_kernel(z_ref, hid_ref, own_ref, r1, r2, r3, ob_ref, ng_ref, nb_ref, z1_ref, low_ref):
    rows = pl.ds(pl.multiple_of(z_ref[0] * BLK, BLK), BLK)
    z1 = hid_ref[rows, :].astype(F32) + own_ref[...] + ob_ref[0:1, :]
    for r in (r1, r2, r3):
        z1 = z1 + r[...].astype(F32)
    z1_ref[...] = z1
    normed, _ = moments(z1)
    low_ref[...] = (normed * ng_ref[0:1, :] + nb_ref[0:1, :]).astype(BF)


def first_norm(z, hidden, own, received, out_biases, norm_gains, norm_biases):
    d = hidden.shape[1]
    return pl.pallas_call(
        first_norm_kernel,
        out_shape=(sds((BLK, d), F32), sds((BLK, d), BF)),
        in_specs=[SM] + [VM] * 8,
        out_specs=(VM,) * 2,
        name="first_norm",
    )(z, hidden, own, *received, out_biases, norm_gains, norm_biases)


def feed_fwd_kernel(x0, x1, x2, x3, wu_ref, bu_ref, wd_ref, x_ref, pre_ref, act_ref, own_ref, *send_refs):
    for s, x in enumerate((x0, x1, x2, x3)):
        v = x[...]
        x_ref[block(s), :] = v
        pre = mm(v, wu_ref[...]) + bu_ref[...]
        pre_ref[block(s), :] = pre
        act = (0.5 * pre * (1.0 + lax.erf(pre * INV_ROOT_TWO))).astype(BF)
        act_ref[block(s), :] = act
        part = mm(act, wd_ref[...])
        if s == 0:
            own_ref[...] = part
        else:
            send_refs[s - 1][...] = part.astype(BF)


def feed_fwd(pieces, w_up, b_up, w_down):
    d, f = w_up.shape
    n = len(pieces)
    return pl.pallas_call(
        feed_fwd_kernel,
        out_shape=(sds((n * BLK, d), BF), sds((n * BLK, f), F32), sds((n * BLK, f), BF), sds((BLK, d), F32))
        + (sds((BLK, d), BF),) * (n - 1),
        in_specs=[VM] * (n + 3),
        out_specs=(VM,) * (3 + n),
        name="feed_fwd",
    )(*pieces, w_up, b_up, w_down)


def second_norm_kernel(
    len_ref, z_ref, z1_ref, own_ref, r1, r2, r3, cot_ref, ob_ref, ng_ref, nb_ref,
    out_ref, grad_ref, low_ref, sums_ref,
):
    start = pl.multiple_of(z_ref[0] * BLK, BLK)
    first_normed, _ = moments(z1_ref[...])
    first = first_normed * ng_ref[0:1, :] + nb_ref[0:1, :]
    feed = own_ref[...]
    for r in (r1, r2, r3):
        feed = feed + r[...].astype(F32)
    normed, inv_std = moments(first + feed + ob_ref[1:2, :])
    valid = lax.broadcasted_iota(jnp.int32, (BLK, 1), 0) + start < len_ref[0]
    second = normed * ng_ref[1:2, :] + nb_ref[1:2, :]
    out_ref[...] = jnp.where(valid, second, 0.0).astype(BF)
    grad_out = jnp.where(valid, cot_ref[pl.ds(start, BLK), :].astype(F32), 0.0)
    second_grad = norm_back(grad_out, normed, inv_std, ng_ref[1:2, :])
    grad_ref[...] = second_grad
    low_ref[...] = second_grad.astype(BF)
    sums_ref[0:1, :] = colsum(grad_out * normed)
    sums_ref[1:2, :] = colsum(grad_out)
    sums_ref[2:3, :] = colsum(second_grad)
    sums_ref[3:8, :] = jnp.zeros_like(sums_ref[3:8, :])


def second_norm(seq_len, z, z1, own, received, cotangent, out_biases, norm_gains, norm_biases):
    d = z1.shape[1]
    return pl.pallas_call(
        second_norm_kernel,
        out_shape=(sds((BLK, d), BF), sds((BLK, d), F32), sds((BLK, d), BF), sds((8, d), F32)),
        in_specs=[SM, SM] + [VM] * 9,
        out_specs=(VM,) * 4,
        name="second_norm",
    )(seq_len, z, z1, own, *received, cotangent, out_biases, norm_gains, norm_biases)


def feed_bwd_kernel(y0, y1, y2, y3, pre_ref, wu_ref, wd_ref, y_ref, gp_ref, gb_ref, own_ref, *send_refs):
    total = None
    for s, y in enumerate((y0, y1, y2, y3)):
        v = y[...]
        y_ref[block(s), :] = v
        grad_act = mm(v, wd_ref[...], 1, 1)
        pre = pre_ref[block(s), :]
        slope = 0.5 * (1.0 + lax.erf(pre * INV_ROOT_TWO)) + pre * jnp.exp(-0.5 * pre * pre) * INV_ROOT_TWO_PI
        grad_pre = (grad_act * slope).astype(BF)
        gp_ref[block(s), :] = grad_pre
        c = colsum(grad_pre.astype(F32))
        total = c if total is None else total + c
        part = mm(grad_pre, wu_ref[...], 1, 1)
        if s == 0:
            own_ref[...] = part
        else:
            send_refs[s - 1][...] = part.astype(BF)
    gb_ref[...] = total


def feed_bwd(pieces, pre_act, w_up, w_down):
    d, f = w_up.shape
    n = len(pieces)
    return pl.pallas_call(
        feed_bwd_kernel,
        out_shape=(sds((n * BLK, d), BF), sds((n * BLK, f), BF), sds((1, f), F32), sds((BLK, d), F32))
        + (sds((BLK, d), BF),) * (n - 1),
        in_specs=[VM] * (n + 3),
        out_specs=(VM,) * (3 + n),
        name="feed_bwd",
    )(*pieces, pre_act, w_up, w_down)


def feed_weights_kernel(x_ref, act_ref, y_ref, gp_ref, out_ref):
    f = act_ref.shape[1]
    d = x_ref.shape[1]
    out_ref[0:f, :] = mm(act_ref[...], y_ref[...], 0, 0).astype(BF)
    out_ref[f : f + d, :] = mm(x_ref[...], gp_ref[...], 0, 0).astype(BF)


def split_rows(rows, count=TAIL):
    high = [r.astype(BF) for r in rows]
    low = [(r - h.astype(F32)).astype(BF) for r, h in zip(rows, high)]
    pad = jnp.zeros((count - 2 * len(rows), rows[0].shape[1]), F32)
    return jnp.concatenate([v.astype(F32) for v in high + low] + [pad], 0).astype(BF)


def join_rows(block_of_rows, count):
    full = block_of_rows.astype(F32)
    return full[:count] + full[count : 2 * count]


def feed_weights(x, act, y, grad_pre):
    d = x.shape[1]
    f = act.shape[1]
    return pl.pallas_call(
        feed_weights_kernel,
        out_shape=sds((f + d, d), BF),
        in_specs=[VM] * 4,
        out_specs=VM,
        name="feed_weights",
    )(x, act, y, grad_pre)


def first_back_kernel(z1_ref, sg_ref, own_ref, r1, r2, r3, sums_ref, ng_ref, fg_ref, low_ref):
    grad_in = sg_ref[...] + own_ref[...]
    for r in (r1, r2, r3):
        grad_in = grad_in + r[...].astype(F32)
    normed, inv_std = moments(z1_ref[...])
    first_grad = norm_back(grad_in, normed, inv_std, ng_ref[0:1, :])
    fg_ref[...] = first_grad
    low_ref[0:BLK, :] = first_grad.astype(BF)
    low_ref[BLK:, :] = split_rows(
        [colsum(grad_in * normed), sums_ref[0:1, :], colsum(grad_in), sums_ref[1:2, :], colsum(first_grad), sums_ref[2:3, :]]
    )


def first_back(z1, second_grad, own, received, sums, norm_gains):
    d = z1.shape[1]
    return pl.pallas_call(
        first_back_kernel,
        out_shape=(sds((BLK, d), F32), sds((BLK + TAIL, d), BF)),
        in_specs=[VM] * 8,
        out_specs=(VM,) * 2,
        name="first_back",
    )(z1, second_grad, own, *received, sums, norm_gains)


def attn_bwd_kernel(
    z_ref, y0, y1, y2, y3, ctx_ref, qkv_ref, tt_ref, pt_ref, idx_ref, wo_ref, gb_ref,
    g_ref, dpos_ref, small_ref, y_s, do_s, dp_s, ds_s, dt_s, *, heads,
):
    n = idx_ref.shape[1] // 2
    z = z_ref[0]
    sums = None
    for s, y in enumerate((y0, y1, y2, y3)):
        y_s[pl.ds(pl.multiple_of(((z + NB - s) % NB) * BLK, BLK), BLK), :] = y[0:BLK, :]
        extra = y[BLK:, :].astype(F32)
        sums = extra if sums is None else sums + extra
    width = heads * HEAD_DIM
    y_all = y_s[...]
    do_all = mm(y_all, wo_ref[...], 1, 1).astype(BF)
    for h in range(heads):
        do_s[h] = do_all[:, h * HEAD_DIM : (h + 1) * HEAD_DIM]
    ctx = jnp.concatenate([ctx_ref[h] for h in range(heads)], 1)
    small_ref[0:width, :] = mm(ctx, y_all, 0, 0).astype(BF)
    small_ref[width:, :] = split_rows(
        [sums[i : i + 1, :] + sums[6 + i : 7 + i, :] for i in range(6)] + [gb_ref[...]], small_ref.shape[0] - width
    )
    flip = anti()

    def head(h, carry):
        do = do_s[h]
        total = None
        for b in range(NB):
            dp = mm(qkv_ref[4, h, block(b), :], do, 1, 1)
            dp_s[block(b), :] = dp
            d = colsum(dp * pt_ref[h, block(b), :].astype(F32))
            total = d if total is None else total + d
        q = qkv_ref[0, h]
        k = qkv_ref[3, h]
        for c in range(2):
            dt_s[c, h] = jnp.zeros((HEAD_DIM, 2 * SLOT), F32)
        for b in range(NB):
            w = slice(b * BLK, b * BLK + WIN)
            p = pt_ref[h, block(b), :]
            gv = mm(p, do).astype(BF)
            dsf = p.astype(F32) * (dp_s[block(b), :] - total)
            ds_s[:, block(b)] = dsf.T.astype(BF)
            u = unskew(dsf).astype(BF)
            gk = ((mm(dsf.astype(BF), q) + mm(u, tt_ref[1, h, :, w], 1, 1)) * SCALE).astype(BF)
            g_ref[1, h, block(NB - 1 - b), :] = mm(flip, gk).astype(BF)
            g_ref[2, h, block(NB - 1 - b), :] = mm(flip, gv).astype(BF)
            dt_s[1, h, :, w] += mm(k[block(b), :], u, 0, 0)
        for b in range(NB):
            w = slice(b * BLK, b * BLK + WIN)
            ds = ds_s[block(b), :]
            u = unskew(ds.astype(F32)).astype(BF)
            g_ref[0, h, block(b), :] = ((mm(ds, k) + mm(u, tt_ref[2, h, :, w], 1, 1)) * SCALE).astype(BF)
            dt_s[0, h, :, w] += mm(q[block(b), :], u, 0, 0)
        return carry

    lax.fori_loop(0, heads, head, 0)
    pos = lax.broadcasted_iota(jnp.int32, (n, 2 * SLOT), 0)
    hot = (pos == idx_ref[1:2, :]).astype(F32).astype(BF)
    for c in range(2):
        d = jnp.concatenate([dt_s[1 - c, h] for h in range(heads)], 0) * SCALE
        dpos_ref[c] = mm(hot, d.astype(BF), 1, 1).astype(BF)


def attn_bwd(z, pieces, ctx, qkv, tt, pt, idx, w_out, grad_b_up):
    heads = ctx.shape[0]
    d = w_out.shape[1]
    n = idx.shape[1] // 2
    return pl.pallas_call(
        functools.partial(attn_bwd_kernel, heads=heads),
        out_shape=(
            sds((3, heads, SLOT, HEAD_DIM), BF),
            sds((2, n, heads * HEAD_DIM), BF),
            sds((heads * HEAD_DIM + 4 * TAIL, d), BF),
        ),
        in_specs=[SM] + [VM] * 11,
        out_specs=(VM,) * 3,
        scratch_shapes=[
            pltpu.VMEM((SLOT, d), BF),
            pltpu.VMEM((heads, SLOT, HEAD_DIM), BF),
            pltpu.VMEM((SLOT, SLOT), F32),
            pltpu.VMEM((SLOT, SLOT), BF),
            pltpu.VMEM((2, heads, HEAD_DIM, 2 * SLOT), F32),
        ],
        name="attn_bwd",
    )(z, *pieces, ctx, qkv, tt, pt, idx, w_out, grad_b_up)


def input_grads_kernel(
    z_ref, g_ref, dpos_ref, hid_ref, tab_ref, tg_ref, tb_ref, w_ref,
    gw_ref, own_ref, *rest, heads,
):
    send_refs = rest[: NB - 1]
    e_s = rest[NB - 1]
    d = hid_ref.shape[1]
    z = z_ref[0]
    normed, _ = moments(tab_ref[...].astype(F32))
    table_low = (normed * tg_ref[...] + tb_ref[...]).astype(BF)
    hid = hid_ref[...]
    biases = []
    for c in range(3):
        g = jnp.concatenate([g_ref[c, h] for h in range(heads)], 1)
        part = mm(hid, g, 0, 0)
        bias = colsum(g.astype(F32))
        if c < 2:
            part = part + mm(table_low, dpos_ref[c], 0, 0)
            bias = bias + colsum(dpos_ref[c].astype(F32))
        gw_ref[c * d : (c + 1) * d, :] = part.astype(BF)
        biases.append(bias)
    gw_ref[3 * d :, :] = split_rows(biases, gw_ref.shape[0] - 3 * d)
    e_s[...] = mm(dpos_ref[0], w_ref[0], 1, 1) + mm(dpos_ref[1], w_ref[1], 1, 1)
    e = e_s[...]
    tail = split_rows([colsum(e * normed), colsum(e)])
    for s in range(NB):
        rows = pl.ds(pl.multiple_of(((z + s) % NB) * BLK, BLK), BLK)
        part = None
        for c in range(3):
            g = jnp.concatenate([g_ref[c, h, rows, :] for h in range(heads)], 1)
            t = mm(g, w_ref[c], 1, 1)
            part = t if part is None else part + t
        dest = own_ref if s == 0 else send_refs[s - 1]
        dest[0:BLK, :] = part.astype(BF)
        dest[BLK : 2 * BLK, :] = e_s[rows, :].astype(BF)
        dest[2 * BLK :, :] = tail


def input_grads(z, g, dpos, hidden, rel_table, rel_gain, rel_bias, w_qkv):
    heads = g.shape[1]
    d = hidden.shape[1]
    return pl.pallas_call(
        functools.partial(input_grads_kernel, heads=heads),
        out_shape=(sds((3 * d + 8 * TAIL, heads * HEAD_DIM), BF),) + (sds((2 * BLK + TAIL, d), BF),) * NB,
        in_specs=[SM] + [VM] * 7,
        out_specs=(VM,) * (1 + NB),
        scratch_shapes=[pltpu.VMEM(rel_table.shape, F32)],
        name="input_grads",
    )(z, g, dpos, hidden, rel_table, rel_gain, rel_bias, w_qkv)


def finish_kernel(fg_ref, p0, p1, p2, p3, dh_ref, table_ref):
    total = p0[...].astype(F32)
    for p in (p1, p2, p3):
        total = total + p[...].astype(F32)
    dh_ref[...] = (fg_ref[...] + total[0:BLK]).astype(BF)
    table_ref[0:BLK, :] = total[BLK : 2 * BLK].astype(BF)
    table_ref[BLK:, :] = split_rows(
        [total[2 * BLK + i : 2 * BLK + i + 1] + total[2 * BLK + 2 + i : 2 * BLK + 3 + i] for i in range(2)],
        2 * TAIL,
    )


def finish(first_grad, parts):
    d = first_grad.shape[1]
    return pl.pallas_call(
        finish_kernel,
        out_shape=(sds((BLK, d), BF), sds((BLK + 2 * TAIL, d), BF)),
        in_specs=[VM] * 5,
        out_specs=(VM,) * 2,
        name="finish",
    )(first_grad, *parts)


def cyclic(n, s):
    return [(i, (i + s) % n) for i in range(n)]


def spread(piece):
    n = lax.axis_size("mp")
    return [piece] + [lax.ppermute(piece, "mp", cyclic(n, s)) for s in range(1, n)]


def give_back(parts):
    n = lax.axis_size("mp")
    return [lax.ppermute(p, "mp", cyclic(n, n - s)) for s, p in zip(range(1, n), parts)]


def hand_out(parts):
    n = lax.axis_size("mp")
    return [lax.ppermute(p, "mp", cyclic(n, s)) for s, p in zip(range(1, n), parts)]


def dp_levels():
    n = lax.axis_size("dp")
    bits = n.bit_length() - 1
    others = list(range(1, bits))
    return n, [(0, 0)] + list(zip(others, others[::-1]))


def dp_sum(x):
    n, levels = dp_levels()
    me = lax.axis_index("dp")
    shape = x.shape
    x = x.reshape((-1,) + shape[-1:])
    trail = []
    for even, odd in levels:
        pairs = [(i, i ^ (1 << (odd if i & 1 else even))) for i in range(n)]
        if x.shape[0] % (2 * TAIL):
            x = (x.astype(F32) + lax.ppermute(x, "dp", pairs).astype(F32)).astype(BF)
            continue
        bit = jnp.where(me & 1, (me >> odd) & 1, (me >> even) & 1)
        halves = x.reshape((2, x.shape[0] // 2) + x.shape[1:])
        kept = lax.dynamic_index_in_dim(halves, bit, 0, keepdims=False)
        sent = lax.dynamic_index_in_dim(halves, 1 - bit, 0, keepdims=False)
        got = lax.ppermute(sent, "dp", pairs)
        x = (kept.astype(F32) + got.astype(F32)).astype(BF)
        trail.append((pairs, bit))
    for pairs, bit in reversed(trail):
        got = lax.ppermute(x, "dp", pairs)
        x = jnp.where(bit == 0, jnp.concatenate([x, got], 0), jnp.concatenate([got, x], 0))
    return x.reshape(shape)


def per_device(
    hidden, cotangent, seq_lens, w_qkv, b_qkv, w_out, out_biases, w_up, b_up, w_down,
    rel_table, norm_gains, norm_biases, rel_gain, rel_bias,
):
    z = lax.axis_index("mp").astype(jnp.int32).reshape(1)
    d = hidden.shape[1]
    f = w_up.shape[1]
    idx = jnp.asarray(index_rows(rel_table.shape[0] // 2))
    gain_row, bias_row = rel_gain[None], rel_bias[None]
    ctx, qkv, tt, pt, own, *sends = attn_fwd(
        seq_lens, z, hidden, w_qkv, b_qkv, rel_table, gain_row, bias_row, idx, w_out
    )
    z1, first_low = first_norm(z, hidden, own, hand_out(sends), out_biases, norm_gains, norm_biases)
    x, pre_act, act, own, *sends = feed_fwd(spread(first_low), w_up, b_up[None], w_down)
    output, second_grad, second_low, sums = second_norm(
        seq_lens, z, z1, own, give_back(sends), cotangent, out_biases, norm_gains, norm_biases
    )
    y, grad_pre, grad_b_up, own, *sends = feed_bwd(spread(second_low), pre_act, w_up, w_down)
    received = give_back(sends)
    feed_grads = dp_sum(feed_weights(x, act, y, grad_pre))
    first_grad, first_grad_low = first_back(z1, second_grad, own, received, sums, norm_gains)
    g, dpos, small = attn_bwd(z, spread(first_grad_low), ctx, qkv, tt, pt, idx, w_out, grad_b_up)
    small = dp_sum(small)
    qkv_grads, own, *sends = input_grads(z, g, dpos, hidden, rel_table, gain_row, bias_row, w_qkv)
    qkv_grads = dp_sum(qkv_grads)
    d_hidden, table = finish(first_grad, [own] + hand_out(sends))
    table = dp_sum(table)

    sum_w_down = feed_grads[:f].astype(F32)
    sum_w_up = feed_grads[f : f + d].astype(F32)
    width = ctx.shape[0] * HEAD_DIM
    sum_w_out = small[:width].astype(F32)
    vectors = join_rows(small[width:], 7)
    norms = vectors[:6]
    sum_b_up = vectors[6]
    sum_w_qkv = qkv_grads[: 3 * d].astype(F32).reshape(3, d, width)
    sum_b_qkv = join_rows(qkv_grads[3 * d :], 3)
    share = lax.dynamic_slice_in_dim(rel_table, z[0] * BLK, BLK, 0).astype(F32)
    normed, inv_std = moments(share)
    d_rel_table = norm_back(table[:BLK].astype(F32), normed, inv_std, rel_gain)
    vectors = lax.dynamic_slice_in_dim(join_rows(table[BLK:], 2), z[0] * width, width, 1)
    return (
        output,
        d_hidden,
        sum_w_qkv,
        sum_b_qkv,
        sum_w_out,
        norms[4:6],
        sum_w_up,
        sum_b_up,
        sum_w_down,
        d_rel_table,
        norms[0:2],
        norms[2:4],
        vectors[0],
        vectors[1],
    )


def solution(mesh):
    in_specs = (
        P("dp", None),
        P("dp", None),
        P("dp"),
        P(None, None, "mp"),
        P(None, "mp"),
        P("mp", None),
        P(),
        P(None, "mp"),
        P("mp"),
        P("mp", None),
        P(),
        P(),
        P(),
        P(),
        P(),
    )
    out_specs = (
        P(("dp", "mp"), None),
        P(("dp", "mp"), None),
        P(None, None, "mp"),
        P(None, "mp"),
        P("mp", None),
        P(),
        P(None, "mp"),
        P("mp"),
        P("mp", None),
        P("mp", None),
        P(),
        P(),
        P("mp"),
        P("mp"),
    )
    return jax.shard_map(
        per_device, mesh=mesh, in_specs=in_specs, out_specs=out_specs, check_vma=False
    )
```

```python
import functools
import math

import jax
import jax.numpy as jnp
import numpy as np
from jax import lax
from jax.experimental import pallas as pl
from jax.experimental.pallas import tpu as pltpu
from jax.sharding import PartitionSpec as P

HEAD_DIM = 64
SLOT = 512
BLK = 128
NB = SLOT // BLK
WIN = SLOT + BLK
EPS = 1e-07
INV_ROOT_TWO = 0.7071067811865476
INV_ROOT_TWO_PI = 0.3989422804014327
SCALE = 1.0 / math.sqrt(3 * HEAD_DIM)
TAIL = 16
Z, LEN, CORE, BIT1, BIT2, SHARD = range(6)
BF = jnp.bfloat16
F32 = jnp.float32
VM = pl.BlockSpec(memory_space=pltpu.VMEM)
SM = pl.BlockSpec(memory_space=pltpu.SMEM)


def sds(shape, dtype):
    return jax.ShapeDtypeStruct(shape, dtype)


def bucket_index(span_len, buckets):
    middle = buckets // 2
    offsets = np.arange(-(span_len - 1), span_len)
    signs = np.sign(offsets)
    magnitude = np.where(
        (offsets < middle) & (offsets > -middle), middle - 1, np.abs(offsets)
    )
    logged = (
        np.ceil(np.log(magnitude / middle) / np.log((span_len - 1) / middle) * (middle - 1))
        + middle
    )
    logged = np.minimum(logged, buckets - 1)
    return np.where(magnitude <= middle, offsets, logged * signs).astype(np.int64) + buckets


def index_rows(buckets):
    by_offset = bucket_index(SLOT, buckets)
    entry = np.arange(2 * SLOT)

    def pick(r):
        return by_offset[np.clip(r, -(SLOT - 1), SLOT - 1) + SLOT - 1]

    return np.stack([pick(SLOT - 1 - entry), pick(entry - (SLOT - 1))]).astype(np.int32)


def mm(a, b, ca=1, cb=0):
    return lax.dot_general(a, b, (((ca,), (cb,)), ((), ())), preferred_element_type=F32)


def skew(x):
    return pltpu.roll(x, WIN - (BLK - 1), 1, stride=1, stride_axis=0)[:, :SLOT]


def unskew(x):
    padded = jnp.concatenate([x, jnp.zeros((BLK, BLK), x.dtype)], 1)
    return pltpu.roll(padded, 0, 1, stride=1, stride_axis=0)


def anti():
    a = lax.broadcasted_iota(jnp.int32, (BLK, BLK), 0)
    b = lax.broadcasted_iota(jnp.int32, (BLK, BLK), 1)
    return (a + b == BLK - 1).astype(F32).astype(BF)


def block(b):
    return slice(b * BLK, (b + 1) * BLK)


def moments(values):
    centered = values - jnp.mean(values, axis=-1, keepdims=True)
    inv_std = lax.rsqrt(jnp.mean(centered * centered, axis=-1, keepdims=True) + EPS)
    return centered * inv_std, inv_std


def norm_back(grad_in, normed, inv_std, gain_row):
    scaled = grad_in * gain_row
    return inv_std * (
        scaled
        - jnp.mean(scaled, axis=-1, keepdims=True)
        - normed * jnp.mean(scaled * normed, axis=-1, keepdims=True)
    )


def row(ref):
    return ref[...].reshape(1, -1)


def colsum(x):
    return jnp.sum(x, axis=0, keepdims=True)


def attn_fwd_kernel(
    ids_ref, hid_ref, w_ref, b_ref, tab_ref, tg_ref, tb_ref, idx_ref, wo_ref,
    ctx_ref, qkv_ref, tt_ref, pt_ref, own_ref, *rest, heads,
):
    send_refs = rest[: NB - 1]
    at_s, st_s, p_s = rest[NB - 1 :]
    normed, _ = moments(tab_ref[...].astype(F32))
    table_low = (normed * row(tg_ref) + row(tb_ref)).astype(BF)
    rows = table_low.shape[0]
    hid = hid_ref[...]
    flip = anti()
    for c in range(3):
        r = (mm(hid, w_ref[c], 1, 1) + b_ref[c : c + 1, :]).astype(BF)
        for h in range(heads):
            qkv_ref[c, h] = r[:, h * HEAD_DIM : (h + 1) * HEAD_DIM]
        if c:
            for b in range(NB):
                back = mm(flip, r[block(NB - 1 - b)]).astype(BF)
                for h in range(heads):
                    qkv_ref[2 + c, h, block(b), :] = back[:, h * HEAD_DIM : (h + 1) * HEAD_DIM]
    pos = lax.broadcasted_iota(jnp.int32, (rows, 2 * SLOT), 0)
    key_query = [
        (mm(table_low, w_ref[1 - c], 1, 1) + b_ref[1 - c : 2 - c, :]).astype(BF) for c in range(2)
    ]
    hot = [(pos == idx_ref[c : c + 1, :]).astype(F32).astype(BF) for c in range(2)]
    for c, (source, order) in enumerate(((0, 0), (1, 1), (0, 1))):
        spread = mm(key_query[source], hot[order], 0, 0).astype(BF)
        for h in range(heads):
            tt_ref[c, h] = spread[h * HEAD_DIM : (h + 1) * HEAD_DIM, :]
    length = ids_ref[LEN]

    def head(h, carry):
        for b in range(NB):
            w = slice((NB - 1 - b) * BLK, (NB - 1 - b) * BLK + WIN)
            a = skew(mm(qkv_ref[0, h, block(b), :], tt_ref[0, h, :, w]))
            at_s[:, block(b)] = a.T
        q = qkv_ref[0, h]
        peak = None
        for b in range(NB):
            w = slice((NB - 1 - b) * BLK, (NB - 1 - b) * BLK + WIN)
            kb = qkv_ref[1, h, block(b), :]
            s = (mm(kb, q, 1, 1) + skew(mm(kb, tt_ref[1, h, :, w])) + at_s[block(b), :]) * SCALE
            j = lax.broadcasted_iota(jnp.int32, s.shape, 0) + b * BLK
            s = jnp.where(j < length, s, -1e30)
            st_s[block(b), :] = s
            m = jnp.max(s, axis=0, keepdims=True)
            peak = m if peak is None else jnp.maximum(peak, m)
        total = None
        for b in range(NB):
            e = jnp.exp(st_s[block(b), :] - peak)
            st_s[block(b), :] = e
            d = colsum(e)
            total = d if total is None else total + d
        share = 1.0 / total
        for b in range(NB):
            p = (st_s[block(b), :] * share).astype(BF)
            p_s[block(b), :] = p
            pt_ref[h, block(NB - 1 - b), :] = mm(flip, p).astype(BF)
        c = mm(qkv_ref[2, h], p_s[...], 0, 0)
        at_s[:, 0:HEAD_DIM] = c.T
        ctx_ref[h] = at_s[:, 0:HEAD_DIM].astype(BF)
        return carry

    lax.fori_loop(0, heads, head, 0)
    z = ids_ref[Z]
    for s in range(NB):
        rows = pl.ds(pl.multiple_of((z ^ s) * BLK, BLK), BLK)
        part = mm(jnp.concatenate([ctx_ref[h, rows, :] for h in range(heads)], 1), wo_ref[...])
        if s == 0:
            own_ref[...] = part
        else:
            send_refs[s - 1][...] = part.astype(BF)


def attn_fwd(ids, hidden, w_qkv, b_qkv, rel_table, rel_gain, rel_bias, idx, w_out):
    heads = w_qkv.shape[1] // HEAD_DIM
    d = hidden.shape[1]
    return pl.pallas_call(
        functools.partial(attn_fwd_kernel, heads=heads),
        out_shape=(
            sds((heads, SLOT, HEAD_DIM), BF),
            sds((5, heads, SLOT, HEAD_DIM), BF),
            sds((3, heads, HEAD_DIM, 2 * SLOT), BF),
            sds((heads, SLOT, SLOT), BF),
            sds((BLK, d), F32),
        )
        + (sds((BLK, d), BF),) * (NB - 1),
        in_specs=[SM] + [VM] * 8,
        out_specs=(VM,) * (4 + NB),
        scratch_shapes=[
            pltpu.VMEM((SLOT, SLOT), F32),
            pltpu.VMEM((SLOT, SLOT), F32),
            pltpu.VMEM((SLOT, SLOT), BF),
        ],
        name="attn_fwd",
    )(ids, hidden, w_qkv, b_qkv, rel_table, rel_gain, rel_bias, idx, w_out)


def first_norm_kernel(ids_ref, hid_ref, own_ref, r1, r2, r3, ob_ref, ng_ref, nb_ref, z1_ref, low_ref):
    rows = pl.ds(pl.multiple_of(ids_ref[Z] * BLK, BLK), BLK)
    z1 = hid_ref[rows, :].astype(F32) + own_ref[...] + ob_ref[0:1, :]
    for r in (r1, r2, r3):
        z1 = z1 + r[...].astype(F32)
    z1_ref[...] = z1
    normed, _ = moments(z1)
    low_ref[...] = (normed * ng_ref[0:1, :] + nb_ref[0:1, :]).astype(BF)


def first_norm(ids, hidden, own, received, out_biases, norm_gains, norm_biases):
    d = hidden.shape[1]
    return pl.pallas_call(
        first_norm_kernel,
        out_shape=(sds((BLK, d), F32), sds((BLK, d), BF)),
        in_specs=[SM] + [VM] * 8,
        out_specs=(VM,) * 2,
        name="first_norm",
    )(ids, hidden, own, *received, out_biases, norm_gains, norm_biases)


def feed_fwd_kernel(x0, x1, x2, x3, wu_ref, bu_ref, wd_ref, x_ref, pre_ref, act_ref, own_ref, *send_refs):
    for s, x in enumerate((x0, x1, x2, x3)):
        v = x[...]
        x_ref[block(s), :] = v
        pre = mm(v, wu_ref[...]) + row(bu_ref)
        pre_ref[block(s), :] = pre
        act = (0.5 * pre * (1.0 + lax.erf(pre * INV_ROOT_TWO))).astype(BF)
        act_ref[block(s), :] = act
        part = mm(act, wd_ref[...])
        if s == 0:
            own_ref[...] = part
        else:
            send_refs[s - 1][...] = part.astype(BF)


def feed_fwd(pieces, w_up, b_up, w_down):
    d, f = w_up.shape
    n = len(pieces)
    return pl.pallas_call(
        feed_fwd_kernel,
        out_shape=(sds((n * BLK, d), BF), sds((n * BLK, f), F32), sds((n * BLK, f), BF), sds((BLK, d), F32))
        + (sds((BLK, d), BF),) * (n - 1),
        in_specs=[VM] * (n + 3),
        out_specs=(VM,) * (3 + n),
        name="feed_fwd",
    )(*pieces, w_up, b_up, w_down)


def second_norm_kernel(
    ids_ref, z1_ref, own_ref, r1, r2, r3, cot_ref, ob_ref, ng_ref, nb_ref,
    out_ref, grad_ref, low_ref, sums_ref,
):
    start = pl.multiple_of(ids_ref[Z] * BLK, BLK)
    first_normed, _ = moments(z1_ref[...])
    first = first_normed * ng_ref[0:1, :] + nb_ref[0:1, :]
    feed = own_ref[...]
    for r in (r1, r2, r3):
        feed = feed + r[...].astype(F32)
    normed, inv_std = moments(first + feed + ob_ref[1:2, :])
    valid = lax.broadcasted_iota(jnp.int32, (BLK, 1), 0) + start < ids_ref[LEN]
    second = normed * ng_ref[1:2, :] + nb_ref[1:2, :]
    out_ref[...] = jnp.where(valid, second, 0.0).astype(BF)
    grad_out = jnp.where(valid, cot_ref[pl.ds(start, BLK), :].astype(F32), 0.0)
    second_grad = norm_back(grad_out, normed, inv_std, ng_ref[1:2, :])
    grad_ref[...] = second_grad
    low_ref[...] = second_grad.astype(BF)
    sums_ref[0:1, :] = colsum(grad_out * normed)
    sums_ref[1:2, :] = colsum(grad_out)
    sums_ref[2:3, :] = colsum(second_grad)
    sums_ref[3:8, :] = jnp.zeros_like(sums_ref[3:8, :])


def second_norm(ids, z1, own, received, cotangent, out_biases, norm_gains, norm_biases):
    d = z1.shape[1]
    return pl.pallas_call(
        second_norm_kernel,
        out_shape=(sds((BLK, d), BF), sds((BLK, d), F32), sds((BLK, d), BF), sds((8, d), F32)),
        in_specs=[SM] + [VM] * 9,
        out_specs=(VM,) * 4,
        name="second_norm",
    )(ids, z1, own, *received, cotangent, out_biases, norm_gains, norm_biases)


def feed_bwd_kernel(y0, y1, y2, y3, pre_ref, wu_ref, wd_ref, y_ref, gp_ref, gb_ref, own_ref, *send_refs):
    total = None
    for s, y in enumerate((y0, y1, y2, y3)):
        v = y[...]
        y_ref[block(s), :] = v
        grad_act = mm(v, wd_ref[...], 1, 1)
        pre = pre_ref[block(s), :]
        slope = 0.5 * (1.0 + lax.erf(pre * INV_ROOT_TWO)) + pre * jnp.exp(-0.5 * pre * pre) * INV_ROOT_TWO_PI
        grad_pre = (grad_act * slope).astype(BF)
        gp_ref[block(s), :] = grad_pre
        c = colsum(grad_pre.astype(F32))
        total = c if total is None else total + c
        part = mm(grad_pre, wu_ref[...], 1, 1)
        if s == 0:
            own_ref[...] = part
        else:
            send_refs[s - 1][...] = part.astype(BF)
    gb_ref[...] = total


def feed_bwd(pieces, pre_act, w_up, w_down):
    d, f = w_up.shape
    n = len(pieces)
    return pl.pallas_call(
        feed_bwd_kernel,
        out_shape=(sds((n * BLK, d), BF), sds((n * BLK, f), BF), sds((1, f), F32), sds((BLK, d), F32))
        + (sds((BLK, d), BF),) * (n - 1),
        in_specs=[VM] * (n + 3),
        out_specs=(VM,) * (3 + n),
        name="feed_bwd",
    )(*pieces, pre_act, w_up, w_down)


def feed_weights_kernel(ids_ref, x_ref, act_ref, y_ref, gp_ref, keep_ref, send_ref):
    core = ids_ref[CORE]

    def down(ref):
        ref[...] = mm(act_ref[...], y_ref[...], 0, 0).astype(BF)

    def up(ref):
        ref[...] = mm(x_ref[...], gp_ref[...], 0, 0).astype(BF)

    @pl.when(core == 0)
    def _():
        up(send_ref)
        down(keep_ref)

    @pl.when(core != 0)
    def _():
        down(send_ref)
        up(keep_ref)


def feed_weights(ids, x, act, y, grad_pre):
    d = x.shape[1]
    assert act.shape[1] == d
    return pl.pallas_call(
        feed_weights_kernel,
        out_shape=(sds((d, d), BF),) * 2,
        in_specs=[SM] + [VM] * 4,
        out_specs=(VM,) * 2,
        name="feed_weights",
    )(ids, x, act, y, grad_pre)


def split_rows(rows, count=TAIL):
    high = [r.astype(BF) for r in rows]
    low = [(r - h.astype(F32)).astype(BF) for r, h in zip(rows, high)]
    pad = jnp.zeros((count - 2 * len(rows), rows[0].shape[1]), F32)
    return jnp.concatenate([v.astype(F32) for v in high + low] + [pad], 0).astype(BF)


def join_rows(block_of_rows, count):
    full = block_of_rows.astype(F32)
    return full[:count] + full[count : 2 * count]


def add_split_kernel(ids_ref, kept_ref, got_ref, keep_ref, send_ref, *, which):
    half = keep_ref.shape[0]
    bit = ids_ref[which]

    def add(at):
        rows = pl.ds(pl.multiple_of(at * half, TAIL), half)
        return (kept_ref[rows, :].astype(F32) + got_ref[rows, :].astype(F32)).astype(BF)

    send_ref[...] = add(1 - bit)
    keep_ref[...] = add(bit)


def add_split(ids, kept, got, which):
    rows, d = kept.shape
    return pl.pallas_call(
        functools.partial(add_split_kernel, which=which),
        out_shape=(sds((rows // 2, d), BF),) * 2,
        in_specs=[SM] + [VM] * 2,
        out_specs=(VM,) * 2,
        name="add_split",
    )(ids, kept, got)


def widen_kernel(ids_ref, mine_ref, got_ref, low_ref, high_ref):
    core = ids_ref[CORE]

    @pl.when(core == 0)
    def _():
        low_ref[...] = mine_ref[...].astype(F32)
        high_ref[...] = got_ref[...].astype(F32)

    @pl.when(core != 0)
    def _():
        low_ref[...] = got_ref[...].astype(F32)
        high_ref[...] = mine_ref[...].astype(F32)


def widen(ids, mine, got):
    return pl.pallas_call(
        widen_kernel,
        out_shape=(sds(mine.shape, F32),) * 2,
        in_specs=[SM] + [VM] * 2,
        out_specs=(VM,) * 2,
        name="widen",
    )(ids, mine, got)


def first_back_kernel(z1_ref, sg_ref, own_ref, r1, r2, r3, sums_ref, ng_ref, fg_ref, low_ref):
    grad_in = sg_ref[...] + own_ref[...]
    for r in (r1, r2, r3):
        grad_in = grad_in + r[...].astype(F32)
    normed, inv_std = moments(z1_ref[...])
    first_grad = norm_back(grad_in, normed, inv_std, ng_ref[0:1, :])
    fg_ref[...] = first_grad
    low_ref[0:BLK, :] = first_grad.astype(BF)
    low_ref[BLK:, :] = split_rows(
        [colsum(grad_in * normed), sums_ref[0:1, :], colsum(grad_in), sums_ref[1:2, :], colsum(first_grad), sums_ref[2:3, :]]
    )


def first_back(z1, second_grad, own, received, sums, norm_gains):
    d = z1.shape[1]
    return pl.pallas_call(
        first_back_kernel,
        out_shape=(sds((BLK, d), F32), sds((BLK + TAIL, d), BF)),
        in_specs=[VM] * 8,
        out_specs=(VM,) * 2,
        name="first_back",
    )(z1, second_grad, own, *received, sums, norm_gains)


def attn_bwd_kernel(
    ids_ref, y0, y1, y2, y3, ctx_ref, qkv_ref, tt_ref, pt_ref, idx_ref, wo_ref, gb_ref,
    hid_ref, tab_ref, tg_ref, tb_ref,
    g_ref, keep_ref, send_ref, y_s, do_s, dp_s, ds_s, dt_s, full_s, *, heads,
):
    n = idx_ref.shape[1] // 2
    width = heads * HEAD_DIM
    d = wo_ref.shape[1]
    z = ids_ref[Z]
    sums = None
    for s, y in enumerate((y0, y1, y2, y3)):
        y_s[pl.ds(pl.multiple_of((z ^ s) * BLK, BLK), BLK), :] = y[0:BLK, :]
        extra = y[BLK:, :].astype(F32)
        sums = extra if sums is None else sums + extra
    do_all = mm(y_s[...], wo_ref[...], 1, 1).astype(BF)
    for h in range(heads):
        do_s[h] = do_all[:, h * HEAD_DIM : (h + 1) * HEAD_DIM]
    flip = anti()

    def head(h, carry):
        do = do_s[h]
        total = None
        for b in range(NB):
            dp = mm(qkv_ref[4, h, block(b), :], do, 1, 1)
            dp_s[block(b), :] = dp
            part = colsum(dp * pt_ref[h, block(b), :].astype(F32))
            total = part if total is None else total + part
        q = qkv_ref[0, h]
        k = qkv_ref[3, h]
        for c in range(2):
            dt_s[c, h] = jnp.zeros((HEAD_DIM, 2 * SLOT), F32)
        for b in range(NB):
            w = slice(b * BLK, b * BLK + WIN)
            p = pt_ref[h, block(b), :]
            gv = mm(p, do).astype(BF)
            dsf = p.astype(F32) * (dp_s[block(b), :] - total)
            ds_s[:, block(b)] = dsf.T.astype(BF)
            u = unskew(dsf).astype(BF)
            gk = ((mm(dsf.astype(BF), q) + mm(u, tt_ref[1, h, :, w], 1, 1)) * SCALE).astype(BF)
            g_ref[1, h, block(NB - 1 - b), :] = mm(flip, gk).astype(BF)
            g_ref[2, h, block(NB - 1 - b), :] = mm(flip, gv).astype(BF)
            dt_s[0, h, :, w] += mm(k[block(b), :], u, 0, 0)
        for b in range(NB):
            w = slice(b * BLK, b * BLK + WIN)
            ds = ds_s[block(b), :]
            u = unskew(ds.astype(F32)).astype(BF)
            g_ref[0, h, block(b), :] = ((mm(ds, k) + mm(u, tt_ref[2, h, :, w], 1, 1)) * SCALE).astype(BF)
            dt_s[1, h, :, w] += mm(q[block(b), :], u, 0, 0)
        return carry

    lax.fori_loop(0, heads, head, 0)
    pos = lax.broadcasted_iota(jnp.int32, (n, 2 * SLOT), 0)
    hot = (pos == idx_ref[1:2, :]).astype(F32).astype(BF)
    tables = jnp.concatenate([dt_s[c, h] for c in range(2) for h in range(heads)], 0) * SCALE
    dpos = mm(hot, tables.astype(BF), 1, 1).astype(BF)
    normed, _ = moments(tab_ref[...].astype(F32))
    table_low = (normed * row(tg_ref) + row(tb_ref)).astype(BF)
    hid = hid_ref[...]
    grads = []
    for c in range(3):
        g = jnp.concatenate([g_ref[c, h] for h in range(heads)], 1)
        part = mm(g, hid, 0, 0)
        bias = colsum(g.astype(F32))
        if c < 2:
            t = dpos[:, c * width : (c + 1) * width]
            part = part + mm(t, table_low, 0, 0)
            bias = bias + colsum(t.astype(F32))
        full_s[c * width : (c + 1) * width, :] = part.astype(BF)
        grads.append(jnp.concatenate([bias, jnp.zeros((1, d - width), F32)], 1))
    ctx = jnp.concatenate([ctx_ref[h] for h in range(heads)], 1)
    full_s[3 * width : 4 * width, :] = mm(ctx, y_s[...], 0, 0).astype(BF)
    full_s[4 * width :, :] = split_rows(
        [sums[i : i + 1, :] + sums[6 + i : 7 + i, :] for i in range(6)] + [gb_ref[...]] + grads,
        full_s.shape[0] - 4 * width,
    )
    core = ids_ref[CORE]
    strip = n // (8 * NB)
    other = full_s.shape[0] // 8
    total_rows = 2 * strip + other
    for k in range(8):
        at = (k % 4) * total_rows
        left = [dpos[c * BLK + k * strip : c * BLK + (k + 1) * strip, :] for c in range(NB)]

        def put(ref, k=k, at=at, left=left):
            ref[at : at + strip, :] = jnp.concatenate([left[0], left[2]], 1)
            ref[at + strip : at + 2 * strip, :] = jnp.concatenate([left[1], left[3]], 1)
            ref[at + 2 * strip : at + total_rows, :] = full_s[k * other : (k + 1) * other, :]

        @pl.when(core == k // 4)
        def _(put=put):
            put(keep_ref)

        @pl.when(core != k // 4)
        def _(put=put):
            put(send_ref)


def attn_bwd(ids, pieces, ctx, qkv, tt, pt, idx, w_out, grad_b_up, hidden, rel_table, rel_gain, rel_bias):
    heads = ctx.shape[0]
    d = w_out.shape[1]
    n = idx.shape[1] // 2
    width = heads * HEAD_DIM
    full = 4 * width + 8 * TAIL
    half = (full + 8 * 2 * (n // (8 * NB))) // 2
    return pl.pallas_call(
        functools.partial(attn_bwd_kernel, heads=heads),
        out_shape=(sds((3, heads, SLOT, HEAD_DIM), BF), sds((half, d), BF), sds((half, d), BF)),
        in_specs=[SM] + [VM] * 15,
        out_specs=(VM,) * 3,
        scratch_shapes=[
            pltpu.VMEM((SLOT, d), BF),
            pltpu.VMEM((heads, SLOT, HEAD_DIM), BF),
            pltpu.VMEM((SLOT, SLOT), F32),
            pltpu.VMEM((SLOT, SLOT), BF),
            pltpu.VMEM((2, heads, HEAD_DIM, 2 * SLOT), F32),
            pltpu.VMEM((full, d), BF),
        ],
        name="attn_bwd",
    )(ids, *pieces, ctx, qkv, tt, pt, idx, w_out, grad_b_up, hidden, rel_table, rel_gain, rel_bias)


def input_parts_kernel(ids_ref, g_ref, w_ref, own_ref, *send_refs, heads):
    z = ids_ref[Z]
    for s in range(NB):
        rows = pl.ds(pl.multiple_of((z ^ s) * BLK, BLK), BLK)
        part = None
        for c in range(3):
            g = jnp.concatenate([g_ref[c, h, rows, :] for h in range(heads)], 1)
            t = mm(g, w_ref[c])
            part = t if part is None else part + t
        if s == 0:
            own_ref[...] = part
        else:
            send_refs[s - 1][...] = part.astype(BF)


def input_parts(ids, g, w_qkv):
    heads = g.shape[1]
    d = w_qkv.shape[2]
    return pl.pallas_call(
        functools.partial(input_parts_kernel, heads=heads),
        out_shape=(sds((BLK, d), F32),) + (sds((BLK, d), BF),) * (NB - 1),
        in_specs=[SM] + [VM] * 2,
        out_specs=(VM,) * NB,
        name="input_parts",
    )(ids, g, w_qkv)


def finish_kernel(fg_ref, own_ref, p1, p2, p3, dh_ref):
    total = fg_ref[...] + own_ref[...]
    for p in (p1, p2, p3):
        total = total + p[...].astype(F32)
    dh_ref[...] = total.astype(BF)


def finish(first_grad, own, parts):
    return pl.pallas_call(
        finish_kernel,
        out_shape=sds(first_grad.shape, BF),
        in_specs=[VM] * 5,
        out_specs=VM,
        name="finish",
    )(first_grad, own, *parts)


def table_rows(ids_ref, tab_ref, strip, chunk):
    at = pl.multiple_of(chunk * BLK + ids_ref[SHARD] * strip, TAIL)
    return moments(tab_ref[pl.ds(at, strip), :].astype(F32))


def table_parts_kernel(ids_ref, kept_ref, got_ref, w_ref, tab_ref, rest_ref, own_ref, s1, s2, s3, e_s, *, strip):
    rows = 2 * strip
    top = (kept_ref[0:rows, :].astype(F32) + got_ref[0:rows, :].astype(F32)).astype(BF)
    rest_ref[...] = (kept_ref[rows:, :].astype(F32) + got_ref[rows:, :].astype(F32)).astype(BF)
    side = top.shape[1] // 2
    width = w_ref.shape[1]
    local = jnp.concatenate([top[:, 0:side], top[:, side:]], 0)
    e = mm(local[:, 0:width], w_ref[0]) + mm(local[:, width : 2 * width], w_ref[1])
    gain = None
    for c in range(NB):
        part = e[c * strip : (c + 1) * strip, :]
        e_s[c] = part
        normed, _ = table_rows(ids_ref, tab_ref, strip, c)
        t = colsum(part * normed)
        gain = t if gain is None else gain + t
    tail = split_rows([gain, colsum(e)])
    z = ids_ref[Z]
    own_ref[0:strip, :] = e_s[z]
    own_ref[strip:, :] = tail.astype(F32)
    for s, ref in ((1, s1), (2, s2), (3, s3)):
        ref[0:strip, :] = e_s[z ^ s].astype(BF)
        ref[strip:, :] = tail


def table_parts(ids, kept, got, w_qkv, rel_table):
    d = kept.shape[1]
    strip = rel_table.shape[0] // (8 * NB)
    return pl.pallas_call(
        functools.partial(table_parts_kernel, strip=strip),
        out_shape=(sds((kept.shape[0] - 2 * strip, d), BF), sds((strip + TAIL, d), F32))
        + (sds((strip + TAIL, d), BF),) * (NB - 1),
        in_specs=[SM] + [VM] * 4,
        out_specs=(VM,) * (1 + NB),
        scratch_shapes=[pltpu.VMEM((NB, strip, d), F32)],
        name="table_parts",
    )(ids, kept, got, w_qkv, rel_table)


def table_back_kernel(ids_ref, own_ref, r1, r2, r3, tab_ref, tg_ref, out_ref, *, strip):
    total = own_ref[...]
    for r in (r1, r2, r3):
        total = total + r[...].astype(F32)
    normed, inv_std = table_rows(ids_ref, tab_ref, strip, ids_ref[Z])
    out_ref[0:strip, :] = norm_back(total[0:strip], normed, inv_std, row(tg_ref)).astype(BF)
    out_ref[strip:, :] = split_rows([total[strip + i : strip + i + 1] + total[strip + 2 + i : strip + 3 + i] for i in range(2)])


def table_back(ids, own, received, rel_table, rel_gain):
    strip = rel_table.shape[0] // (8 * NB)
    return pl.pallas_call(
        functools.partial(table_back_kernel, strip=strip),
        out_shape=sds(own.shape, BF),
        in_specs=[SM] + [VM] * 6,
        out_specs=VM,
        name="table_back",
    )(ids, own, *received, rel_table, rel_gain)


def weights_out_kernel(ids_ref, mine_ref, got_ref, qkv_ref, out_ref, rows_ref):
    first = ids_ref[CORE] == 0
    mine = mine_ref[...].astype(F32)
    got = got_ref[...].astype(F32)
    low = jnp.where(first, mine, got)
    high = jnp.where(first, got, mine)
    half = low.shape[0]
    a = qkv_ref.shape[0]
    b = out_ref.shape[0]
    qkv_ref[0:half, :] = low
    qkv_ref[half:, :] = high[0 : a - half]
    out_ref[...] = high[a - half : a - half + b]
    tail = high[a - half + b :]
    rows_ref[0:10, :] = tail[0:10] + tail[10:20]
    rows_ref[10:, :] = jnp.zeros_like(rows_ref[10:, :])


def weights_out(ids, mine, got, width):
    d = mine.shape[1]
    return pl.pallas_call(
        weights_out_kernel,
        out_shape=(sds((3 * width, d), F32), sds((width, d), F32), sds((TAIL, d), F32)),
        in_specs=[SM] + [VM] * 2,
        out_specs=(VM,) * 3,
        name="weights_out",
    )(ids, mine, got)


def table_out_kernel(ids_ref, mine_ref, got_ref, table_ref, rows_ref, *, strip):
    core = ids_ref[CORE]
    piece = strip + TAIL
    total = None
    for i in range(4):
        for ref, who in ((mine_ref, core), (got_ref, 1 - core)):
            at = pl.multiple_of((who * 4 + i) * strip, strip)
            table_ref[pl.ds(at, strip), :] = ref[i * piece : i * piece + strip, :].astype(F32)
            t = ref[i * piece + strip : (i + 1) * piece, :].astype(F32)
            total = t if total is None else total + t
    rows_ref[...] = total[0:8]


def table_out(ids, mine, got, strip):
    d = mine.shape[1]
    return pl.pallas_call(
        functools.partial(table_out_kernel, strip=strip),
        out_shape=(sds((8 * strip, d), F32), sds((8, d), F32)),
        in_specs=[SM] + [VM] * 2,
        out_specs=(VM,) * 2,
        name="table_out",
    )(ids, mine, got)


def spread(piece):
    n = lax.axis_size("mp")
    return [piece] + exchange([piece] * (n - 1))


def exchange(parts):
    n = lax.axis_size("mp")
    return [
        lax.ppermute(p, "mp", [(i, i ^ s) for i in range(n)]) for s, p in zip(range(1, n), parts)
    ]


def dp_bits():
    n = lax.axis_size("dp")
    others = list(range(1, n.bit_length() - 1))
    return n, list(zip(others, others[::-1]))


def swap_core(x):
    return lax.ppermute(x, "dp", [(i, i ^ 1) for i in range(lax.axis_size("dp"))])


def swap(x, level):
    n, bits = dp_bits()
    even, odd = bits[level]
    return lax.ppermute(x, "dp", [(i, i ^ (1 << (odd if i & 1 else even))) for i in range(n)])


def sum_rest(x):
    for level in range(2, len(dp_bits()[1])):
        x = (x.astype(F32) + swap(x, level).astype(F32)).astype(BF)
    return x


def joined(ids, x, level):
    got = swap(x, level)
    return jnp.where(ids[BIT1 + level] == 0, jnp.concatenate([x, got], 0), jnp.concatenate([got, x], 0))


def device_ids(seq_lens):
    me = lax.axis_index("dp").astype(jnp.int32)
    core = me & 1
    _, bits = dp_bits()
    b1, b2 = [jnp.where(core == 0, (me >> even) & 1, (me >> odd) & 1) for even, odd in bits[:2]]
    z = lax.axis_index("mp").astype(jnp.int32)
    return jnp.stack([z, seq_lens[0], core, b1, b2, core * 4 + b1 * 2 + b2])


def per_device(
    hidden, cotangent, seq_lens, w_qkv, b_qkv, w_out, out_biases, w_up, b_up, w_down,
    rel_table, norm_gains, norm_biases, rel_gain, rel_bias,
):
    ids = device_ids(seq_lens)
    width = w_qkv.shape[2]
    strip = rel_table.shape[0] // (8 * NB)
    idx = jnp.asarray(index_rows(rel_table.shape[0] // 2))
    w_qkv = jnp.swapaxes(w_qkv, 1, 2)
    ctx, qkv, tt, pt, own, *sends = attn_fwd(
        ids, hidden, w_qkv, b_qkv, rel_table, rel_gain, rel_bias, idx, w_out
    )
    z1, first_low = first_norm(ids, hidden, own, exchange(sends), out_biases, norm_gains, norm_biases)
    x, pre_act, act, own, *sends = feed_fwd(spread(first_low), w_up, b_up, w_down)
    output, second_grad, second_low, sums = second_norm(
        ids, z1, own, exchange(sends), cotangent, out_biases, norm_gains, norm_biases
    )
    y, grad_pre, grad_b_up, own, *sends = feed_bwd(spread(second_low), pre_act, w_up, w_down)
    received = exchange(sends)
    kept, sent = feed_weights(ids, x, act, y, grad_pre)
    kept, sent = add_split(ids, kept, swap_core(sent), BIT1)
    received, kept, sent = lax.optimization_barrier((received, kept, sent))
    first_grad, first_grad_low = first_back(z1, second_grad, own, received, sums, norm_gains)
    pieces = spread(first_grad_low)
    kept, sent = add_split(ids, kept, swap(sent, 0), BIT2)
    pieces, kept, sent = lax.optimization_barrier((pieces, kept, sent))
    g, keep, send = attn_bwd(
        ids, pieces, ctx, qkv, tt, pt, idx, w_out, grad_b_up, hidden, rel_table, rel_gain, rel_bias
    )
    got = swap_core(send)
    own, *sends = input_parts(ids, g, w_qkv)
    keep, send = add_split(ids, keep, got, BIT1)
    received = exchange(sends)
    keep, send = add_split(ids, keep, swap(send, 0), BIT2)
    rest, table, *parts = table_parts(ids, sum_rest(keep), sum_rest(swap(send, 1)), w_qkv, rel_table)
    table = table_back(ids, table, exchange(parts), rel_table, rel_gain)
    feed = sum_rest((kept.astype(F32) + swap(sent, 1).astype(F32)).astype(BF))
    feed = joined(ids, joined(ids, feed, 1), 0)
    rest = joined(ids, joined(ids, rest, 1), 0)
    table = joined(ids, joined(ids, table, 1), 0)
    sum_w_down, sum_w_up = widen(ids, feed, swap_core(feed))
    sum_w_qkv, sum_w_out, rows = weights_out(ids, rest, swap_core(rest), width)
    d_rel_table, table_sums = table_out(ids, table, swap_core(table), strip)
    d_hidden = finish(first_grad, own, received)
    vectors = lax.dynamic_slice_in_dim(table_sums[0:2] + table_sums[2:4], ids[Z] * width, width, 1)
    return (
        output,
        d_hidden,
        jnp.swapaxes(sum_w_qkv.reshape(3, width, -1), 1, 2),
        rows[7:10, :width],
        sum_w_out,
        rows[4:6],
        sum_w_up,
        rows[6],
        sum_w_down,
        d_rel_table,
        rows[0:2],
        rows[2:4],
        vectors[0],
        vectors[1],
    )


def solution(mesh):
    in_specs = (
        P("dp", None),
        P("dp", None),
        P("dp"),
        P(None, None, "mp"),
        P(None, "mp"),
        P("mp", None),
        P(),
        P(None, "mp"),
        P("mp"),
        P("mp", None),
        P(),
        P(),
        P(),
        P(),
        P(),
    )
    out_specs = (
        P(("dp", "mp"), None),
        P(("dp", "mp"), None),
        P(None, None, "mp"),
        P(None, "mp"),
        P("mp", None),
        P(),
        P(None, "mp"),
        P("mp"),
        P("mp", None),
        P("mp", None),
        P(),
        P(),
        P("mp"),
        P("mp"),
    )
    return jax.shard_map(
        per_device, mesh=mesh, in_specs=in_specs, out_specs=out_specs, check_vma=False
    )
```

```python
import functools
import math

import jax
import jax.numpy as jnp
import numpy as np
from jax import lax
from jax.experimental import pallas as pl
from jax.experimental.pallas import tpu as pltpu
from jax.sharding import PartitionSpec as P


HEAD_DIM = 64
SLOT = 512
BLK = 128
NB = SLOT // BLK
WIN = SLOT + BLK
EPS = 1e-07
INV_ROOT_TWO = 0.7071067811865476
INV_ROOT_TWO_PI = 0.3989422804014327
SCALE = 1.0 / math.sqrt(3 * HEAD_DIM)
TAIL = 16
Z, LEN, CORE, BIT1, BIT2, SHARD = range(6)
BF = jnp.bfloat16
F32 = jnp.float32
VM = pl.BlockSpec(memory_space=pltpu.VMEM)
SM = pl.BlockSpec(memory_space=pltpu.SMEM)
HB = pl.BlockSpec(memory_space=pltpu.HBM)


LIMIT = 24 * 1024 * 1024
FLOPS_PER_US = 1.15e9


def cost(us):
    return pl.CostEstimate(flops=int(us * FLOPS_PER_US), transcendentals=0, bytes_accessed=0)


def sds(shape, dtype):
    return jax.ShapeDtypeStruct(shape, dtype)


def bucket_index(span_len, buckets):
    middle = buckets // 2
    offsets = np.arange(-(span_len - 1), span_len)
    signs = np.sign(offsets)
    magnitude = np.where(
        (offsets < middle) & (offsets > -middle), middle - 1, np.abs(offsets)
    )
    logged = (
        np.ceil(np.log(magnitude / middle) / np.log((span_len - 1) / middle) * (middle - 1))
        + middle
    )
    logged = np.minimum(logged, buckets - 1)
    return np.where(magnitude <= middle, offsets, logged * signs).astype(np.int64) + buckets


def index_rows(buckets):
    by_offset = bucket_index(SLOT, buckets)
    entry = np.arange(2 * SLOT)

    def pick(r):
        return by_offset[np.clip(r, -(SLOT - 1), SLOT - 1) + SLOT - 1]

    return np.stack([pick(SLOT - 1 - entry), pick(entry - (SLOT - 1))]).astype(np.int32)


def mm(a, b, ca=1, cb=0):
    return lax.dot_general(a, b, (((ca,), (cb,)), ((), ())), preferred_element_type=F32)


def skew(x):
    return pltpu.roll(x, WIN - (BLK - 1), 1, stride=1, stride_axis=0)[:, :SLOT]


def unskew(x):
    padded = jnp.concatenate([x, jnp.zeros((BLK, BLK), x.dtype)], 1)
    return pltpu.roll(padded, 0, 1, stride=1, stride_axis=0)


def anti():
    a = lax.broadcasted_iota(jnp.int32, (BLK, BLK), 0)
    b = lax.broadcasted_iota(jnp.int32, (BLK, BLK), 1)
    return (a + b == BLK - 1).astype(F32).astype(BF)


def block(b):
    return slice(b * BLK, (b + 1) * BLK)


def moments(values):
    centered = values - jnp.mean(values, axis=-1, keepdims=True)
    inv_std = lax.rsqrt(jnp.mean(centered * centered, axis=-1, keepdims=True) + EPS)
    return centered * inv_std, inv_std


def norm_back(grad_in, normed, inv_std, gain_row):
    scaled = grad_in * gain_row
    return inv_std * (
        scaled
        - jnp.mean(scaled, axis=-1, keepdims=True)
        - normed * jnp.mean(scaled * normed, axis=-1, keepdims=True)
    )


def row(ref):
    return ref[...].reshape(1, -1)


def colsum(x):
    return jnp.sum(x, axis=0, keepdims=True)


def attn_fwd_kernel(
    ids_ref, tab_hbm, tg_hbm, tb_hbm, w_hbm, b_hbm, idx_hbm, hid_hbm, wo_hbm,
    ctx_ref, qkv_ref, tt_ref, pt_ref, own_ref, *rest, heads,
):
    send_refs = rest[: NB - 1]
    at_s, st_s, p_s, sems, *loaded = rest[NB - 1 :]
    tab_ref, tg_ref, tb_ref, w_ref, b_ref, idx_ref, hid_ref, wo_ref = loaded
    sources = (tab_hbm, tg_hbm, tb_hbm, w_hbm, b_hbm, idx_hbm, hid_hbm, wo_hbm)
    copies = [pltpu.make_async_copy(a, b, sems.at[i]) for i, (a, b) in enumerate(zip(sources, loaded))]
    for c in copies:
        c.start()
    for c in copies[:3]:
        c.wait()
    normed, _ = moments(tab_ref[...].astype(F32))
    table_low = (normed * row(tg_ref) + row(tb_ref)).astype(BF)
    rows = table_low.shape[0]
    for c in copies[3:7]:
        c.wait()
    hid = hid_ref[...]
    flip = anti()
    for c in range(3):
        r = (mm(hid, w_ref[c], 1, 1) + b_ref[c : c + 1, :]).astype(BF)
        for h in range(heads):
            qkv_ref[c, h] = r[:, h * HEAD_DIM : (h + 1) * HEAD_DIM]
        if c:
            for b in range(NB):
                back = mm(flip, r[block(NB - 1 - b)]).astype(BF)
                for h in range(heads):
                    qkv_ref[2 + c, h, block(b), :] = back[:, h * HEAD_DIM : (h + 1) * HEAD_DIM]
    pos = lax.broadcasted_iota(jnp.int32, (rows, 2 * SLOT), 0)
    key_query = [
        (mm(table_low, w_ref[1 - c], 1, 1) + b_ref[1 - c : 2 - c, :]).astype(BF) for c in range(2)
    ]
    hot = [(pos == idx_ref[c : c + 1, :]).astype(F32).astype(BF) for c in range(2)]
    for c, (source, order) in enumerate(((0, 0), (1, 1), (0, 1))):
        spread = mm(key_query[source], hot[order], 0, 0).astype(BF)
        for h in range(heads):
            tt_ref[c, h] = spread[h * HEAD_DIM : (h + 1) * HEAD_DIM, :]
    length = ids_ref[LEN]

    def head(h, carry):
        for b in range(NB):
            w = slice((NB - 1 - b) * BLK, (NB - 1 - b) * BLK + WIN)
            a = skew(mm(qkv_ref[0, h, block(b), :], tt_ref[0, h, :, w]))
            at_s[:, block(b)] = a.T
        q = qkv_ref[0, h]
        peak = None
        for b in range(NB):
            w = slice((NB - 1 - b) * BLK, (NB - 1 - b) * BLK + WIN)
            kb = qkv_ref[1, h, block(b), :]
            s = (mm(kb, q, 1, 1) + skew(mm(kb, tt_ref[1, h, :, w])) + at_s[block(b), :]) * SCALE
            j = lax.broadcasted_iota(jnp.int32, s.shape, 0) + b * BLK
            s = jnp.where(j < length, s, -1e30)
            st_s[block(b), :] = s
            m = jnp.max(s, axis=0, keepdims=True)
            peak = m if peak is None else jnp.maximum(peak, m)
        total = None
        for b in range(NB):
            e = jnp.exp(st_s[block(b), :] - peak)
            st_s[block(b), :] = e
            d = colsum(e)
            total = d if total is None else total + d
        share = 1.0 / total
        for b in range(NB):
            p = (st_s[block(b), :] * share).astype(BF)
            p_s[block(b), :] = p
            pt_ref[h, block(NB - 1 - b), :] = mm(flip, p).astype(BF)
        c = mm(qkv_ref[2, h], p_s[...], 0, 0)
        at_s[:, 0:HEAD_DIM] = c.T
        ctx_ref[h] = at_s[:, 0:HEAD_DIM].astype(BF)
        return carry

    lax.fori_loop(0, heads, head, 0)
    z = ids_ref[Z]
    copies[7].wait()
    for s in range(NB):
        rows = pl.ds(pl.multiple_of((z ^ s) * BLK, BLK), BLK)
        part = mm(jnp.concatenate([ctx_ref[h, rows, :] for h in range(heads)], 1), wo_ref[...])
        if s == 0:
            own_ref[...] = part
        else:
            send_refs[s - 1][...] = part.astype(BF)


def attn_fwd(ids, hidden, w_qkv, b_qkv, rel_table, rel_gain, rel_bias, idx, w_out):
    heads = w_qkv.shape[1] // HEAD_DIM
    d = hidden.shape[1]
    loads = (rel_table, rel_gain, rel_bias, w_qkv, b_qkv, idx, hidden, w_out)
    return pl.pallas_call(
        functools.partial(attn_fwd_kernel, heads=heads),
        out_shape=(
            sds((heads, SLOT, HEAD_DIM), BF),
            sds((5, heads, SLOT, HEAD_DIM), BF),
            sds((3, heads, HEAD_DIM, 2 * SLOT), BF),
            sds((heads, SLOT, SLOT), BF),
            sds((BLK, d), F32),
        )
        + (sds((BLK, d), BF),) * (NB - 1),
        in_specs=[SM] + [HB] * len(loads),
        out_specs=(VM,) * (4 + NB),
        scratch_shapes=[
            pltpu.VMEM((SLOT, SLOT), F32),
            pltpu.VMEM((SLOT, SLOT), F32),
            pltpu.VMEM((SLOT, SLOT), BF),
            pltpu.SemaphoreType.DMA((len(loads),)),
        ]
        + [pltpu.VMEM(v.shape, v.dtype) for v in loads],
        name="attn_fwd",
        cost_estimate=cost(9.5),
        compiler_params=pltpu.CompilerParams(vmem_limit_bytes=LIMIT),
    )(ids, *[pltpu.with_memory_space_constraint(v, pltpu.HBM) for v in loads])


def first_norm_kernel(ids_ref, hid_ref, own_ref, r1, r2, r3, ob_ref, ng_ref, nb_ref, z1_ref, low_ref):
    rows = pl.ds(pl.multiple_of(ids_ref[Z] * BLK, BLK), BLK)
    z1 = hid_ref[rows, :].astype(F32) + own_ref[...] + ob_ref[0:1, :]
    for r in (r1, r2, r3):
        z1 = z1 + r[...].astype(F32)
    z1_ref[...] = z1
    normed, _ = moments(z1)
    low_ref[...] = (normed * ng_ref[0:1, :] + nb_ref[0:1, :]).astype(BF)


def first_norm(ids, hidden, own, received, out_biases, norm_gains, norm_biases):
    d = hidden.shape[1]
    return pl.pallas_call(
        first_norm_kernel,
        out_shape=(sds((BLK, d), F32), sds((BLK, d), BF)),
        in_specs=[SM] + [VM] * 8,
        out_specs=(VM,) * 2,
        name="first_norm",
        cost_estimate=cost(0.8),
        compiler_params=pltpu.CompilerParams(vmem_limit_bytes=LIMIT),
    )(ids, hidden, own, *received, out_biases, norm_gains, norm_biases)


def weight_slice_kernel(ids_ref, wu_hbm, wd_hbm, bu_ref, out_ref, sem):
    rows = out_ref.shape[0] - TAIL
    at = pl.multiple_of((ids_ref[SHARD] & 3) * rows, TAIL)

    def load(ref):
        copy = pltpu.make_async_copy(ref.at[pl.ds(at, rows)], out_ref.at[pl.ds(0, rows)], sem)
        copy.start()
        copy.wait()

    @pl.when(ids_ref[CORE] == 0)
    def _():
        load(wu_hbm)

    @pl.when(ids_ref[CORE] != 0)
    def _():
        load(wd_hbm)

    out_ref[rows:, :] = split_rows([row(bu_ref)])


def weight_slice(ids, w_up, w_down, b_up):
    d = w_up.shape[0]
    assert w_up.shape == w_down.shape == (d, d)
    hbm = [pltpu.with_memory_space_constraint(v, pltpu.HBM) for v in (w_up, w_down)]
    return pl.pallas_call(
        weight_slice_kernel,
        out_shape=sds((d // 4 + TAIL, d), BF),
        in_specs=[SM, HB, HB, VM],
        out_specs=VM,
        scratch_shapes=[pltpu.SemaphoreType.DMA],
        name="weight_slice",
        cost_estimate=cost(1.5),
        compiler_params=pltpu.CompilerParams(vmem_limit_bytes=LIMIT),
    )(ids, *hbm, b_up)


def pick_weights_kernel(ids_ref, wu_ref, wd_ref, bu_ref, mine_ref, got_ref, up_ref, down_ref, bias_ref):
    piece = mine_ref.shape[0] // 4
    rows = piece - TAIL

    @pl.when(ids_ref[CORE] == 0)
    def _():
        up_ref[...] = wu_ref[...]
        down_ref[...] = wd_ref[...]
        bias_ref[...] = row(bu_ref)

    @pl.when(ids_ref[CORE] != 0)
    def _():
        for k in range(4):
            up_ref[k * rows : (k + 1) * rows, :] = got_ref[k * piece : k * piece + rows, :]
            down_ref[k * rows : (k + 1) * rows, :] = mine_ref[k * piece : k * piece + rows, :]
        bias_ref[...] = join_rows(mine_ref[rows:piece, :], 1)


def pick_weights(ids, w_up, w_down, b_up, mine, got):
    d = w_up.shape[0]
    return pl.pallas_call(
        pick_weights_kernel,
        out_shape=(sds((d, d), BF), sds((d, d), BF), sds((1, d), F32)),
        in_specs=[SM] + [VM] * 5,
        out_specs=(VM,) * 3,
        name="pick_weights",
        cost_estimate=cost(1.5),
        compiler_params=pltpu.CompilerParams(vmem_limit_bytes=LIMIT),
    )(ids, w_up, w_down, b_up, mine, got)


def feed_fwd_kernel(x0, x1, x2, x3, wu_ref, bu_ref, wd_ref, x_ref, pre_ref, act_ref, own_ref, send_ref):
    for s, x in enumerate((x0, x1, x2, x3)):
        v = x[...]
        x_ref[block(s), :] = v
        pre = mm(v, wu_ref[...]) + bu_ref[...]
        pre_ref[block(s), :] = pre
        act = (0.5 * pre * (1.0 + lax.erf(pre * INV_ROOT_TWO))).astype(BF)
        act_ref[block(s), :] = act
        part = mm(act, wd_ref[...])
        if s < 2:
            own_ref[block(s), :] = part
        else:
            send_ref[block(s - 2), :] = part.astype(BF)


def feed_fwd(pieces, w_up, b_up, w_down):
    d, f = w_up.shape
    n = len(pieces)
    return pl.pallas_call(
        feed_fwd_kernel,
        out_shape=(
            sds((n * BLK, d), BF),
            sds((n * BLK, f), F32),
            sds((n * BLK, f), BF),
            sds((2 * BLK, d), F32),
            sds((2 * BLK, d), BF),
        ),
        in_specs=[VM] * (n + 3),
        out_specs=(VM,) * 5,
        name="feed_fwd",
        cost_estimate=cost(1.9),
        compiler_params=pltpu.CompilerParams(vmem_limit_bytes=LIMIT),
    )(*pieces, w_up, b_up, w_down)


def pair_add_kernel(own_ref, got_ref, sum_ref, send_ref, *, start):
    total = own_ref[...] + got_ref[...].astype(F32)
    sum_ref[...] = total
    send_ref[...] = total[start:].astype(BF)


def pair_add(own, got, start):
    rows, d = own.shape
    return pl.pallas_call(
        functools.partial(pair_add_kernel, start=start),
        out_shape=(sds((rows, d), F32), sds((rows - start, d), BF)),
        in_specs=[VM] * 2,
        out_specs=(VM,) * 2,
        name="pair_add",
        cost_estimate=cost(0.7),
        compiler_params=pltpu.CompilerParams(vmem_limit_bytes=LIMIT),
    )(own, got)


def second_norm_kernel(
    ids_ref, z1_ref, x_ref, sum_ref, got_ref, cot_ref, ob_ref, ng_ref, nb_ref,
    out_ref, grad_ref, low_ref, sums_ref,
):
    for who in range(2):
        start = pl.multiple_of((ids_ref[Z] ^ who) * BLK, BLK)
        if who == 0:
            first_normed, _ = moments(z1_ref[...])
            first = first_normed * ng_ref[0:1, :] + nb_ref[0:1, :]
        else:
            first = x_ref[...].astype(F32)
        feed = sum_ref[block(who), :] + got_ref[block(1 - who), :].astype(F32)
        normed, inv_std = moments(first + feed + ob_ref[1:2, :])
        valid = lax.broadcasted_iota(jnp.int32, (BLK, 1), 0) + start < ids_ref[LEN]
        grad_out = jnp.where(valid, cot_ref[pl.ds(start, BLK), :].astype(F32), 0.0)
        second_grad = norm_back(grad_out, normed, inv_std, ng_ref[1:2, :])
        low_ref[block(who), :] = second_grad.astype(BF)
        if who == 0:
            second = normed * ng_ref[1:2, :] + nb_ref[1:2, :]
            out_ref[...] = jnp.where(valid, second, 0.0).astype(BF)
            grad_ref[...] = second_grad
            sums_ref[0:1, :] = colsum(grad_out * normed)
            sums_ref[1:2, :] = colsum(grad_out)
            sums_ref[2:3, :] = colsum(second_grad)
            sums_ref[3:8, :] = jnp.zeros_like(sums_ref[3:8, :])


def second_norm(ids, z1, x, total, got, cotangent, out_biases, norm_gains, norm_biases):
    d = z1.shape[1]
    return pl.pallas_call(
        second_norm_kernel,
        out_shape=(sds((BLK, d), BF), sds((BLK, d), F32), sds((2 * BLK, d), BF), sds((8, d), F32)),
        in_specs=[SM] + [VM] * 8,
        out_specs=(VM,) * 4,
        name="second_norm",
        cost_estimate=cost(2.5),
        compiler_params=pltpu.CompilerParams(vmem_limit_bytes=LIMIT),
    )(ids, z1, x, total, got, cotangent, out_biases, norm_gains, norm_biases)


def feed_bwd_kernel(y0, y1, pre_ref, wu_ref, wd_ref, y_ref, gp_ref, gb_ref, own_ref, send_ref):
    total = None
    for s in range(4):
        v = (y0, y1)[s // 2][block(s % 2), :]
        y_ref[block(s), :] = v
        grad_act = mm(v, wd_ref[...], 1, 1)
        pre = pre_ref[block(s), :]
        slope = 0.5 * (1.0 + lax.erf(pre * INV_ROOT_TWO)) + pre * jnp.exp(-0.5 * pre * pre) * INV_ROOT_TWO_PI
        grad_pre = (grad_act * slope).astype(BF)
        gp_ref[block(s), :] = grad_pre
        c = colsum(grad_pre.astype(F32))
        total = c if total is None else total + c
        part = mm(grad_pre, wu_ref[...], 1, 1)
        if s < 2:
            own_ref[block(s), :] = part
        else:
            send_ref[block(s - 2), :] = part.astype(BF)
    gb_ref[...] = total


def feed_bwd(pairs, pre_act, w_up, w_down):
    d, f = w_up.shape
    n = 4
    return pl.pallas_call(
        feed_bwd_kernel,
        out_shape=(
            sds((n * BLK, d), BF),
            sds((n * BLK, f), BF),
            sds((1, f), F32),
            sds((2 * BLK, d), F32),
            sds((2 * BLK, d), BF),
        ),
        in_specs=[VM] * 5,
        out_specs=(VM,) * 5,
        name="feed_bwd",
        cost_estimate=cost(2.9),
        compiler_params=pltpu.CompilerParams(vmem_limit_bytes=LIMIT),
    )(*pairs, pre_act, w_up, w_down)


def feed_weights_kernel(ids_ref, x_ref, act_ref, y_ref, gp_ref, gb_ref, keep_ref, send_ref, full_s):
    d = x_ref.shape[1]
    quarter = d // 2
    half = quarter // 2
    rows = half + TAIL
    full_s[0:d, :] = mm(act_ref[...], y_ref[...], 0, 0).astype(BF)
    full_s[d : 2 * d, :] = mm(x_ref[...], gp_ref[...], 0, 0).astype(BF)
    bias = split_rows([gb_ref[...]])
    core = ids_ref[CORE]
    for ref, bit in ((keep_ref, ids_ref[BIT1]), (send_ref, 1 - ids_ref[BIT1])):
        for i in range(2):
            source = jnp.where(core == 0, bit * 2 + i, i * 2 + bit)
            for h in range(2):
                at = (2 * i + h) * rows
                from_row = pl.multiple_of(source * quarter + h * half, TAIL)
                ref[at : at + half, :] = full_s[pl.ds(from_row, half), :]
                ref[at + half : at + rows, :] = bias


def feed_weights(ids, x, act, y, grad_pre, grad_b_up):
    d = x.shape[1]
    assert act.shape[1] == d
    rows = 4 * (d // 4 + TAIL)
    return pl.pallas_call(
        feed_weights_kernel,
        out_shape=(sds((rows, d), BF),) * 2,
        in_specs=[SM] + [VM] * 5,
        out_specs=(VM,) * 2,
        scratch_shapes=[pltpu.VMEM((2 * d, d), BF)],
        name="feed_weights",
        cost_estimate=cost(2.5),
        compiler_params=pltpu.CompilerParams(vmem_limit_bytes=LIMIT),
    )(ids, x, act, y, grad_pre, grad_b_up)


def split_rows(rows, count=TAIL):
    high = [r.astype(BF) for r in rows]
    low = [(r - h.astype(F32)).astype(BF) for r, h in zip(rows, high)]
    pad = jnp.zeros((count - 2 * len(rows), rows[0].shape[1]), F32)
    return jnp.concatenate([v.astype(F32) for v in high + low] + [pad], 0).astype(BF)


def join_rows(block_of_rows, count):
    full = block_of_rows.astype(F32)
    return full[:count] + full[count : 2 * count]


def add_split_kernel(ids_ref, kept_ref, got_ref, keep_ref, send_ref, *, which):
    half = keep_ref.shape[0]
    bit = ids_ref[which]

    def add(at):
        rows = pl.ds(pl.multiple_of(at * half, TAIL), half)
        return (kept_ref[rows, :].astype(F32) + got_ref[rows, :].astype(F32)).astype(BF)

    send_ref[...] = add(1 - bit)
    keep_ref[...] = add(bit)


def add_split(ids, kept, got, which):
    rows, d = kept.shape
    return pl.pallas_call(
        functools.partial(add_split_kernel, which=which),
        out_shape=(sds((rows // 2, d), BF),) * 2,
        in_specs=[SM] + [VM] * 2,
        out_specs=(VM,) * 2,
        name="add_split",
        cost_estimate=cost(0.7),
        compiler_params=pltpu.CompilerParams(vmem_limit_bytes=LIMIT),
    )(ids, kept, got)


def widen_kernel(ids_ref, mine_ref, got_ref, down_ref, up_ref, bias_ref):
    core = ids_ref[CORE]
    rows = mine_ref.shape[0] // 4
    half = rows - TAIL
    quarter = 2 * half

    def put(zero, one):
        for a, out in enumerate((down_ref, up_ref)):
            for b in range(2):
                at = (a * 2 + b) * rows
                out[b * quarter : b * quarter + half, :] = zero[at : at + half, :].astype(F32)
                at = (b * 2 + a) * rows
                out[b * quarter + half : (b + 1) * quarter, :] = one[at : at + half, :].astype(F32)

    @pl.when(core == 0)
    def _():
        put(mine_ref, got_ref)

    @pl.when(core != 0)
    def _():
        put(got_ref, mine_ref)

    bias_ref[...] = join_rows(mine_ref[half:rows, :], 1)


def widen(ids, mine, got):
    d = mine.shape[1]
    return pl.pallas_call(
        widen_kernel,
        out_shape=(sds((d, d), F32), sds((d, d), F32), sds((1, d), F32)),
        in_specs=[SM] + [VM] * 2,
        out_specs=(VM,) * 3,
        name="widen",
        cost_estimate=cost(3.2),
        compiler_params=pltpu.CompilerParams(vmem_limit_bytes=LIMIT),
    )(ids, mine, got)


def shard_half_kernel(ids_ref, kept_ref, got_ref, half_ref, send_ref):
    half = half_ref.shape[0]
    total = kept_ref[...].astype(F32) + got_ref[...].astype(F32)
    half_ref[...] = total[0:half].astype(BF)
    send_ref[...] = total[half:].astype(BF)


def shard_half(ids, kept, got):
    rows, d = kept.shape
    return pl.pallas_call(
        shard_half_kernel,
        out_shape=(sds((rows // 2, d), BF),) * 2,
        in_specs=[SM] + [VM] * 2,
        out_specs=(VM,) * 2,
        name="shard_half",
        cost_estimate=cost(0.7),
        compiler_params=pltpu.CompilerParams(vmem_limit_bytes=LIMIT),
    )(ids, kept, got)


def first_back_kernel(z1_ref, sg_ref, sum_ref, got_ref, sums_ref, ng_ref, fg_ref, low_ref):
    grad_in = sg_ref[...] + sum_ref[0:BLK, :] + got_ref[...].astype(F32)
    normed, inv_std = moments(z1_ref[...])
    first_grad = norm_back(grad_in, normed, inv_std, ng_ref[0:1, :])
    fg_ref[...] = first_grad
    low_ref[0:BLK, :] = first_grad.astype(BF)
    low_ref[BLK:, :] = split_rows(
        [colsum(grad_in * normed), sums_ref[0:1, :], colsum(grad_in), sums_ref[1:2, :], colsum(first_grad), sums_ref[2:3, :]]
    )


def first_back(z1, second_grad, total, got, sums, norm_gains):
    d = z1.shape[1]
    return pl.pallas_call(
        first_back_kernel,
        out_shape=(sds((BLK, d), F32), sds((BLK + TAIL, d), BF)),
        in_specs=[VM] * 6,
        out_specs=(VM,) * 2,
        name="first_back",
        cost_estimate=cost(0.5),
        compiler_params=pltpu.CompilerParams(vmem_limit_bytes=LIMIT),
    )(z1, second_grad, total, got, sums, norm_gains)


def attn_bwd_kernel(
    ids_ref, y0, y1, y2, y3, ctx_ref, qkv_ref, tt_ref, pt_ref, idx_ref, wo_ref,
    hid_ref, tab_ref, tg_ref, tb_ref,
    g_ref, keep_ref, send_ref, y_s, do_s, dp_s, ds_s, dt_s, full_s, *, heads,
):
    n = idx_ref.shape[1] // 2
    width = heads * HEAD_DIM
    d = wo_ref.shape[1]
    z = ids_ref[Z]
    sums = None
    for s, y in enumerate((y0, y1, y2, y3)):
        y_s[pl.ds(pl.multiple_of((z ^ s) * BLK, BLK), BLK), :] = y[0:BLK, :]
        extra = y[BLK:, :].astype(F32)
        sums = extra if sums is None else sums + extra
    do_all = mm(y_s[...], wo_ref[...], 1, 1).astype(BF)
    for h in range(heads):
        do_s[h] = do_all[:, h * HEAD_DIM : (h + 1) * HEAD_DIM]
    flip = anti()

    def head(h, carry):
        do = do_s[h]
        total = None
        for b in range(NB):
            dp = mm(qkv_ref[4, h, block(b), :], do, 1, 1)
            dp_s[block(b), :] = dp
            part = colsum(dp * pt_ref[h, block(b), :].astype(F32))
            total = part if total is None else total + part
        q = qkv_ref[0, h]
        k = qkv_ref[3, h]
        for c in range(2):
            dt_s[c, h] = jnp.zeros((HEAD_DIM, 2 * SLOT), F32)
        for b in range(NB):
            w = slice(b * BLK, b * BLK + WIN)
            p = pt_ref[h, block(b), :]
            gv = mm(p, do).astype(BF)
            dsf = p.astype(F32) * (dp_s[block(b), :] - total)
            ds_s[:, block(b)] = dsf.T.astype(BF)
            u = unskew(dsf).astype(BF)
            gk = ((mm(dsf.astype(BF), q) + mm(u, tt_ref[1, h, :, w], 1, 1)) * SCALE).astype(BF)
            g_ref[1, h, block(NB - 1 - b), :] = mm(flip, gk).astype(BF)
            g_ref[2, h, block(NB - 1 - b), :] = mm(flip, gv).astype(BF)
            dt_s[0, h, :, w] += mm(k[block(b), :], u, 0, 0)
        for b in range(NB):
            w = slice(b * BLK, b * BLK + WIN)
            ds = ds_s[block(b), :]
            u = unskew(ds.astype(F32)).astype(BF)
            g_ref[0, h, block(b), :] = ((mm(ds, k) + mm(u, tt_ref[2, h, :, w], 1, 1)) * SCALE).astype(BF)
            dt_s[1, h, :, w] += mm(q[block(b), :], u, 0, 0)
        return carry

    lax.fori_loop(0, heads, head, 0)
    pos = lax.broadcasted_iota(jnp.int32, (n, 2 * SLOT), 0)
    hot = (pos == idx_ref[1:2, :]).astype(F32).astype(BF)
    tables = jnp.concatenate([dt_s[c, h] for c in range(2) for h in range(heads)], 0) * SCALE
    dpos = mm(hot, tables.astype(BF), 1, 1).astype(BF)
    normed, _ = moments(tab_ref[...].astype(F32))
    table_low = (normed * row(tg_ref) + row(tb_ref)).astype(BF)
    hid = hid_ref[...]
    grads = []
    for c in range(3):
        g = jnp.concatenate([g_ref[c, h] for h in range(heads)], 1)
        part = mm(g, hid, 0, 0)
        bias = colsum(g.astype(F32))
        if c < 2:
            t = dpos[:, c * width : (c + 1) * width]
            part = part + mm(t, table_low, 0, 0)
            bias = bias + colsum(t.astype(F32))
        full_s[c * width : (c + 1) * width, :] = part.astype(BF)
        grads.append(jnp.concatenate([bias, jnp.zeros((1, d - width), F32)], 1))
    ctx = jnp.concatenate([ctx_ref[h] for h in range(heads)], 1)
    full_s[3 * width : 4 * width, :] = mm(ctx, y_s[...], 0, 0).astype(BF)
    full_s[4 * width :, :] = split_rows(
        [sums[i : i + 1, :] + sums[6 + i : 7 + i, :] for i in range(6)] + grads,
        full_s.shape[0] - 4 * width,
    )
    core = ids_ref[CORE]
    strip = n // (8 * NB)
    other = full_s.shape[0] // 8
    total_rows = 2 * strip + other
    for k in range(8):
        at = (k % 4) * total_rows
        left = [dpos[c * BLK + k * strip : c * BLK + (k + 1) * strip, :] for c in range(NB)]

        def put(ref, k=k, at=at, left=left):
            ref[at : at + strip, :] = jnp.concatenate([left[0], left[2]], 1)
            ref[at + strip : at + 2 * strip, :] = jnp.concatenate([left[1], left[3]], 1)
            ref[at + 2 * strip : at + total_rows, :] = full_s[k * other : (k + 1) * other, :]

        @pl.when(core == k // 4)
        def _(put=put):
            put(keep_ref)

        @pl.when(core != k // 4)
        def _(put=put):
            put(send_ref)


def attn_bwd(ids, pieces, ctx, qkv, tt, pt, idx, w_out, hidden, rel_table, rel_gain, rel_bias):
    heads = ctx.shape[0]
    d = w_out.shape[1]
    n = idx.shape[1] // 2
    width = heads * HEAD_DIM
    full = 4 * width + 8 * TAIL
    half = (full + 8 * 2 * (n // (8 * NB))) // 2
    return pl.pallas_call(
        functools.partial(attn_bwd_kernel, heads=heads),
        out_shape=(sds((3, heads, SLOT, HEAD_DIM), BF), sds((half, d), BF), sds((half, d), BF)),
        in_specs=[SM] + [VM] * 14,
        out_specs=(VM,) * 3,
        scratch_shapes=[
            pltpu.VMEM((SLOT, d), BF),
            pltpu.VMEM((heads, SLOT, HEAD_DIM), BF),
            pltpu.VMEM((SLOT, SLOT), F32),
            pltpu.VMEM((SLOT, SLOT), BF),
            pltpu.VMEM((2, heads, HEAD_DIM, 2 * SLOT), F32),
            pltpu.VMEM((full, d), BF),
        ],
        name="attn_bwd",
        cost_estimate=cost(11),
        compiler_params=pltpu.CompilerParams(vmem_limit_bytes=LIMIT),
    )(ids, *pieces, ctx, qkv, tt, pt, idx, w_out, hidden, rel_table, rel_gain, rel_bias)


def input_parts_kernel(ids_ref, g_ref, w_ref, own_ref, *send_refs, heads):
    z = ids_ref[Z]
    for s in range(NB):
        rows = pl.ds(pl.multiple_of((z ^ s) * BLK, BLK), BLK)
        part = None
        for c in range(3):
            g = jnp.concatenate([g_ref[c, h, rows, :] for h in range(heads)], 1)
            t = mm(g, w_ref[c])
            part = t if part is None else part + t
        if s == 0:
            own_ref[...] = part
        else:
            send_refs[s - 1][...] = part.astype(BF)


def input_parts(ids, g, w_qkv):
    heads = g.shape[1]
    d = w_qkv.shape[2]
    return pl.pallas_call(
        functools.partial(input_parts_kernel, heads=heads),
        out_shape=(sds((BLK, d), F32),) + (sds((BLK, d), BF),) * (NB - 1),
        in_specs=[SM] + [VM] * 2,
        out_specs=(VM,) * NB,
        name="input_parts",
        cost_estimate=cost(2.1),
        compiler_params=pltpu.CompilerParams(vmem_limit_bytes=LIMIT),
    )(ids, g, w_qkv)


def finish_kernel(fg_ref, own_ref, p1, p2, p3, dh_ref):
    total = fg_ref[...] + own_ref[...]
    for p in (p1, p2, p3):
        total = total + p[...].astype(F32)
    dh_ref[...] = total.astype(BF)


def finish(first_grad, own, parts):
    return pl.pallas_call(
        finish_kernel,
        out_shape=sds(first_grad.shape, BF),
        in_specs=[VM] * 5,
        out_specs=VM,
        name="finish",
        cost_estimate=cost(1.0),
        compiler_params=pltpu.CompilerParams(vmem_limit_bytes=LIMIT),
    )(first_grad, own, *parts)


def table_rows(ids_ref, tab_ref, strip, chunk):
    at = pl.multiple_of(chunk * BLK + ids_ref[SHARD] * strip, TAIL)
    return moments(tab_ref[pl.ds(at, strip), :].astype(F32))


def table_parts_kernel(ids_ref, kept_ref, got_ref, w_ref, tab_ref, rest_ref, own_ref, s1, s2, s3, e_s, *, strip):
    rows = 2 * strip
    top = (kept_ref[0:rows, :].astype(F32) + got_ref[0:rows, :].astype(F32)).astype(BF)
    rest_ref[...] = (kept_ref[rows:, :].astype(F32) + got_ref[rows:, :].astype(F32)).astype(BF)
    side = top.shape[1] // 2
    width = w_ref.shape[1]
    local = jnp.concatenate([top[:, 0:side], top[:, side:]], 0)
    e = mm(local[:, 0:width], w_ref[0]) + mm(local[:, width : 2 * width], w_ref[1])
    gain = None
    for c in range(NB):
        part = e[c * strip : (c + 1) * strip, :]
        e_s[c] = part
        normed, _ = table_rows(ids_ref, tab_ref, strip, c)
        t = colsum(part * normed)
        gain = t if gain is None else gain + t
    tail = split_rows([gain, colsum(e)])
    z = ids_ref[Z]
    own_ref[0:strip, :] = e_s[z]
    own_ref[strip:, :] = tail.astype(F32)
    for s, ref in ((1, s1), (2, s2), (3, s3)):
        ref[0:strip, :] = e_s[z ^ s].astype(BF)
        ref[strip:, :] = tail


def table_parts(ids, kept, got, w_qkv, rel_table):
    d = kept.shape[1]
    strip = rel_table.shape[0] // (8 * NB)
    return pl.pallas_call(
        functools.partial(table_parts_kernel, strip=strip),
        out_shape=(sds((kept.shape[0] - 2 * strip, d), BF), sds((strip + TAIL, d), F32))
        + (sds((strip + TAIL, d), BF),) * (NB - 1),
        in_specs=[SM] + [VM] * 4,
        out_specs=(VM,) * (1 + NB),
        scratch_shapes=[pltpu.VMEM((NB, strip, d), F32)],
        name="table_parts",
        cost_estimate=cost(1.5),
        compiler_params=pltpu.CompilerParams(vmem_limit_bytes=LIMIT),
    )(ids, kept, got, w_qkv, rel_table)


def table_back_kernel(ids_ref, own_ref, r1, r2, r3, tab_ref, tg_ref, out_ref, *, strip):
    total = own_ref[...]
    for r in (r1, r2, r3):
        total = total + r[...].astype(F32)
    normed, inv_std = table_rows(ids_ref, tab_ref, strip, ids_ref[Z])
    out_ref[0:strip, :] = norm_back(total[0:strip], normed, inv_std, row(tg_ref)).astype(BF)
    out_ref[strip:, :] = split_rows([total[strip + i : strip + i + 1] + total[strip + 2 + i : strip + 3 + i] for i in range(2)])


def table_back(ids, own, received, rel_table, rel_gain):
    strip = rel_table.shape[0] // (8 * NB)
    return pl.pallas_call(
        functools.partial(table_back_kernel, strip=strip),
        out_shape=sds(own.shape, BF),
        in_specs=[SM] + [VM] * 6,
        out_specs=VM,
        name="table_back",
        cost_estimate=cost(0.8),
        compiler_params=pltpu.CompilerParams(vmem_limit_bytes=LIMIT),
    )(ids, own, *received, rel_table, rel_gain)


def weights_out_kernel(
    ids_ref, mine_ref, got_ref, qkv_ref, out_ref, bqkv_ref, ng_ref, nb_ref, ob_ref
):
    first = ids_ref[CORE] == 0
    mine = mine_ref[...].astype(F32)
    got = got_ref[...].astype(F32)
    low = jnp.where(first, mine, got)
    high = jnp.where(first, got, mine)
    half = low.shape[0]
    a = qkv_ref.shape[0]
    b = out_ref.shape[0]
    qkv_ref[0:half, :] = low
    qkv_ref[half:, :] = high[0 : a - half]
    out_ref[...] = high[a - half : a - half + b]
    tail = high[a - half + b :]
    rows = tail[0:9] + tail[9:18]
    ng_ref[...] = rows[0:2]
    nb_ref[...] = rows[2:4]
    ob_ref[...] = rows[4:6]
    bqkv_ref[...] = rows[6:9, 0 : bqkv_ref.shape[1]]


def weights_out(ids, mine, got, width):
    d = mine.shape[1]
    return pl.pallas_call(
        weights_out_kernel,
        out_shape=(sds((3 * width, d), F32), sds((width, d), F32), sds((3, width), F32))
        + (sds((2, d), F32),) * 3,
        in_specs=[SM] + [VM] * 2,
        out_specs=(VM,) * 6,
        name="weights_out",
        cost_estimate=cost(2.2),
        compiler_params=pltpu.CompilerParams(vmem_limit_bytes=LIMIT),
    )(ids, mine, got)


def table_out_kernel(ids_ref, mine_ref, got_ref, table_ref, gain_ref, bias_ref, *, strip):
    core = ids_ref[CORE]
    piece = strip + TAIL
    total = None
    for i in range(4):
        for ref, who in ((mine_ref, core), (got_ref, 1 - core)):
            at = pl.multiple_of((who * 4 + i) * strip, strip)
            table_ref[pl.ds(at, strip), :] = ref[i * piece : i * piece + strip, :].astype(F32)
            t = ref[i * piece + strip : (i + 1) * piece, :].astype(F32)
            total = t if total is None else total + t
    width = gain_ref.shape[1]
    full = total.shape[1]
    rows = total[0:8] + pltpu.roll(total[0:8], 6, 0)
    mine_first = pltpu.roll(rows, lax.rem(full - ids_ref[Z] * width, full), 1)
    gain_ref[...] = mine_first[0:1, 0:width]
    bias_ref[...] = mine_first[1:2, 0:width]


def table_out(ids, mine, got, strip, width):
    d = mine.shape[1]
    return pl.pallas_call(
        functools.partial(table_out_kernel, strip=strip),
        out_shape=(sds((8 * strip, d), F32), sds((1, width), F32), sds((1, width), F32)),
        in_specs=[SM] + [VM] * 2,
        out_specs=(VM,) * 3,
        name="table_out",
        cost_estimate=cost(1.7),
        compiler_params=pltpu.CompilerParams(vmem_limit_bytes=LIMIT),
    )(ids, mine, got)


def spread(piece):
    n = lax.axis_size("mp")
    return [piece] + exchange([piece] * (n - 1))


def exchange(parts):
    n = lax.axis_size("mp")
    out = []
    for s, p in zip(range(1, n), parts):
        out.append(lax.ppermute(p, "mp", [(i, i ^ s) for i in range(n)]))
    return out


def dp_bits():
    n = lax.axis_size("dp")
    others = list(range(1, n.bit_length() - 1))
    return n, list(zip(others, others[1::-1] + others[2:]))


def swap_core(x):
    return lax.ppermute(x, "dp", [(i, i ^ 1) for i in range(lax.axis_size("dp"))])


def swap_chip(x):
    return lax.ppermute(x, "mp", [(i, i ^ 1) for i in range(lax.axis_size("mp"))])


def swap_side(x):
    return lax.ppermute(x, "mp", [(i, i ^ 2) for i in range(lax.axis_size("mp"))])


def to_other_core(x, core):
    return lax.ppermute(x, "dp", [(i, i ^ 1) for i in range(core, lax.axis_size("dp"), 2)])


def send_home(x):
    n, m = lax.axis_size("dp"), lax.axis_size("mp")
    return lax.ppermute(
        x, ("dp", "mp"), [(i * m + z, (i - 1) * m + (z ^ 2)) for i in range(1, n, 2) for z in range(m)]
    )


def swap(x, level):
    n, bits = dp_bits()
    even, odd = bits[level]
    return lax.ppermute(x, "dp", [(i, i ^ (1 << (odd if i & 1 else even))) for i in range(n)])


def sum_rest(x):
    for level in range(2, len(dp_bits()[1])):
        x = (x.astype(F32) + swap(x, level).astype(F32)).astype(BF)
    return x


def joined(ids, x, level):
    got = swap(x, level)
    return jnp.where(ids[BIT1 + level] == 0, jnp.concatenate([x, got], 0), jnp.concatenate([got, x], 0))


def device_ids(seq_lens):
    me = lax.axis_index("dp").astype(jnp.int32)
    core = me & 1
    _, bits = dp_bits()
    b1, b2 = [jnp.where(core == 0, (me >> even) & 1, (me >> odd) & 1) for even, odd in bits[:2]]
    z = lax.axis_index("mp").astype(jnp.int32)
    return jnp.stack([z, seq_lens[0], core, b1, b2, core * 4 + b1 * 2 + b2])


def per_device(
    hidden, cotangent, seq_lens, w_qkv, b_qkv, w_out, out_biases, w_up, b_up, w_down,
    rel_table, norm_gains, norm_biases, rel_gain, rel_bias,
):
    ids = device_ids(seq_lens)
    width = w_qkv.shape[2]
    strip = rel_table.shape[0] // (8 * NB)
    idx = jnp.asarray(index_rows(rel_table.shape[0] // 2))
    w_qkv = jnp.swapaxes(w_qkv, 1, 2)
    ctx, qkv, tt, pt, own, *sends = attn_fwd(
        ids, hidden, w_qkv, b_qkv, rel_table, rel_gain, rel_bias, idx, w_out
    )
    z1, first_low = first_norm(ids, hidden, own, exchange(sends), out_biases, norm_gains, norm_biases)
    mine = swap_side(weight_slice(ids, w_up, w_down, b_up))
    mine = joined(ids, joined(ids, mine, 1), 0)
    w_up, w_down, b_row = pick_weights(ids, w_up, w_down, b_up, mine, to_other_core(mine, 0))
    near = swap_chip(first_low)
    pieces = [first_low, near, swap_core(first_low), swap_core(near)]
    x, pre_act, act, own, send = feed_fwd(pieces, w_up, b_row, w_down)
    got = swap_core(send)
    total, send = pair_add(own, got, 0)
    output, second_grad, second_low, sums = second_norm(
        ids, z1, near, total, swap_chip(send), cotangent, out_biases, norm_gains, norm_biases
    )
    y, grad_pre, grad_b_up, own, send = feed_bwd([second_low, swap_core(second_low)], pre_act, w_up, w_down)
    got = swap_core(send)
    total, send = pair_add(own, got, BLK)
    got = swap_chip(send)
    kept, sent = feed_weights(ids, x, act, y, grad_pre, grad_b_up)
    first_grad, first_grad_low = first_back(z1, second_grad, total, got, sums, norm_gains)
    pieces = spread(first_grad_low)
    sent = swap(sent, 0)
    kept, sent = add_split(ids, kept, sent, BIT2)
    g, keep, send = attn_bwd(
        ids, pieces, ctx, qkv, tt, pt, idx, w_out, hidden, rel_table, rel_gain, rel_bias
    )
    got = swap_core(send)
    own, *sends = input_parts(ids, g, w_qkv)
    keep, send = add_split(ids, keep, got, BIT1)
    received = exchange(sends)
    send = swap(send, 0)
    keep, send = add_split(ids, keep, send, BIT2)
    rest, table, *parts = table_parts(ids, sum_rest(keep), sum_rest(swap(send, 1)), w_qkv, rel_table)
    table = table_back(ids, table, exchange(parts), rel_table, rel_gain)
    shard = sum_rest((kept.astype(F32) + swap(sent, 1).astype(F32)).astype(BF))
    feed, send = shard_half(ids, shard, send_home(shard))
    got = to_other_core(send, 0)
    feed = jnp.where(ids[CORE] == 0, feed, got)
    feed = joined(ids, joined(ids, feed, 1), 0)
    rest = joined(ids, joined(ids, rest, 1), 0)
    table = joined(ids, joined(ids, table, 1), 0)
    sum_w_down, sum_w_up, sum_b_up = widen(ids, feed, swap_core(feed))
    table_got = swap_core(table)
    rest_got = swap_core(rest)
    sum_w_qkv, sum_w_out, sum_b_qkv, d_gains, d_biases, d_out = weights_out(ids, rest, rest_got, width)
    d_rel_table, d_gain, d_bias = table_out(ids, table, table_got, strip, width)
    d_hidden = finish(first_grad, own, received)
    return (
        output,
        d_hidden,
        jnp.swapaxes(sum_w_qkv.reshape(3, width, -1), 1, 2),
        sum_b_qkv,
        sum_w_out,
        d_out,
        sum_w_up,
        sum_b_up[0],
        sum_w_down,
        d_rel_table,
        d_gains,
        d_biases,
        d_gain[0],
        d_bias[0],
    )


def solution(mesh):
    in_specs = (
        P("dp", None),
        P("dp", None),
        P("dp"),
        P(None, None, "mp"),
        P(None, "mp"),
        P("mp", None),
        P(),
        P(None, "mp"),
        P("mp"),
        P("mp", None),
        P(),
        P(),
        P(),
        P(),
        P(),
    )
    out_specs = (
        P(("dp", "mp"), None),
        P(("dp", "mp"), None),
        P(None, None, "mp"),
        P(None, "mp"),
        P("mp", None),
        P(),
        P(None, "mp"),
        P("mp"),
        P("mp", None),
        P("mp", None),
        P(),
        P(),
        P("mp"),
        P("mp"),
    )
    return jax.shard_map(
        per_device, mesh=mesh, in_specs=in_specs, out_specs=out_specs, check_vma=False
    )
```
